32 devices in a mesh: row: 8 (over y, x, core), col: 4 (over z).
Axes of the slice: x: 2, y: 2, z: 4, core: 2. Of those that a mesh axis runs over, the one named last changes fastest.
Arguments:
- panel: bfloat16 [24576, 256], P('row', 'col'), as said below
- trailing: bfloat16 [24576, 16384], P('row', 'col'), may hold values from -6 to 6
- tile_list: int32 [176], P('row'), may hold values from 0 to 23, as said below
Outputs:
- triangle: float32 [256, 256], replicated
- top_rows: float32 [16384, 256], P('col')
- updated: bfloat16 [22528, 16384], P('row', 'col')
The draws below stay inside these ranges and needn't reach their ends.
Inputs may be any that keep to these rules, and one draw needn't show every extreme that they name: `tile_list`: each aligned block of 22 entries (the entries of one index of row) lists distinct tile numbers of that group's 24 tiles in increasing order and always includes tile 24 - 1. `panel`: the active rows of every row group, and all active rows together, have full column rank with a condition number under 100.
All inputs are finite; a program needn't handle non-finite values.
Results may differ from the reference program's by a relative error of at most 0.0065.
Values may be sent and summed in bfloat16 or wider, within the bound.
No kernel may reach another device: no remote copies, remote signals or barrier semaphores. Data moves between devices by JAX's collectives and lax.ppermute only.
A program may use at most 128 MiB of HBM per device.

```python
import math
import jax
import jax.numpy as jnp
from jax import lax

TILE = 128
PANEL = 256
TRAIL = 16384
TILES_DEV = 24
ACTIVE_DEV = 22
ROWS = 24576
ACT_ALL = 176


def draw_panel(key, part):
    group_rows = TILES_DEV * TILE
    nblocks = ROWS // group_rows
    key_one, key_two = jax.random.split(jax.random.fold_in(key, 11), 2)
    exponent = jax.random.uniform(key_one, (ROWS, 1), jnp.float32)
    row_scale = jnp.exp(exponent * math.log(10.0))
    device_row = (jnp.arange(ROWS) // group_rows).astype(jnp.float32)
    fraction = device_row / max(nblocks - 1, 1)
    rising = jnp.sqrt(1.0 + 2.0 * fraction)
    base_draw = jax.random.normal(key_two, (ROWS, PANEL), jnp.float32)
    values = base_draw * row_scale * rising[:, None] / (4.0 * math.sqrt(ACT_ALL * TILE))
    return values.astype(jnp.bfloat16)


def draw_tile_list(key, part):
    nblocks = ACT_ALL // ACTIVE_DEV
    key_list = jax.random.split(jax.random.fold_in(key, 23), nblocks)

    def one_block(block_key):
        picked = jax.random.permutation(block_key, TILES_DEV - 1)[:ACTIVE_DEV - 1].astype(jnp.int32)
        joined = jnp.concatenate([picked, jnp.full((1,), TILES_DEV - 1, jnp.int32)])
        return jnp.sort(joined).astype(jnp.int32)
    return jax.vmap(one_block)(key_list).reshape(-1).astype(jnp.int32)


def with_spikes(array, key, source, target, parts, factor):
    owner, partner = [(jnp.arange(array.shape[position]) // (array.shape[position] // parts)).reshape([-1 if axis == position else 1 for axis in range(array.ndim)]) for position in (source, target)]
    chosen = jax.random.permutation(key, parts)[partner]
    strong = (owner == chosen) | (owner == (partner + parts // 2) % parts)
    return jnp.where(strong, factor * array, array)


def levels(key, dims, cuts, smallest, top_value):
    gain, own = 1.0, jax.random.fold_in(key, 6)
    for dim, shards_of in cuts:
        steps = jnp.exp(jax.random.uniform(jax.random.fold_in(own, dim), (shards_of,), jnp.float32, smallest / len(cuts), top_value / len(cuts)))
        gain = gain * jnp.repeat(steps, dims[dim] // shards_of).reshape([-1 if axis == dim else 1 for axis in range(len(dims))])
    return gain


def gaussian_with(stream_key, dims, deviation, reach, shards, heavy, kind=jnp.bfloat16):
    drawn = deviation * jax.random.normal(stream_key, dims, jnp.float32)
    if shards:
        drawn = drawn * levels(stream_key, dims, shards, -0.22, 0.18)
    return jnp.clip(with_spikes(drawn, jax.random.fold_in(stream_key, 3), *heavy), -reach, reach).astype(kind)


def setup_inputs(seed: int = 0) -> dict:
    splits = jax.random.split(jax.random.key(seed), 4)
    panel = draw_panel(jax.random.fold_in(splits[3], 71), 0)
    trailing = gaussian_with(splits[1], (ROWS, TRAIL), 1.0, 6.0, ((0, 8), (1, 4)), (0, 1, 8, 2.0))
    tile_list = draw_tile_list(jax.random.fold_in(splits[3], 71), 0)
    return dict(panel=panel, trailing=trailing, tile_list=tile_list)


def select_rows(whole, tile_list):
    nblocks = tile_list.shape[0] // ACTIVE_DEV
    offsets = (jnp.arange(nblocks, dtype=jnp.int32) * TILES_DEV)[:, None]
    tile_index = (tile_list.reshape(nblocks, ACTIVE_DEV).astype(jnp.int32) + offsets).reshape(-1).astype(jnp.int32)
    tiled = whole.reshape(-1, TILE, whole.shape[1])
    return jnp.take(tiled, tile_index, axis=0).reshape(-1, whole.shape[1])

def reference(panel, trailing, tile_list):
    act_panel = select_rows(panel, tile_list)
    act_trail = select_rows(trailing, tile_list)
    gram_matrix = lax.dot_general(act_panel.astype(jnp.float32), act_panel.astype(jnp.float32), (((0,), (0,)), ((), ())), preferred_element_type=jnp.float32)
    lower_factor = jnp.linalg.cholesky(gram_matrix)
    triangle = lower_factor.T
    cross_sum = lax.dot_general(act_trail.astype(jnp.float32), act_panel.astype(jnp.float32), (((0,), (0,)), ((), ())), preferred_element_type=jnp.float32)
    top_rows = jax.scipy.linalg.solve_triangular(lower_factor, cross_sum.T, lower=True).T
    coeff = jax.scipy.linalg.solve_triangular(lower_factor, top_rows.T, lower=True, trans=1).T.astype(jnp.bfloat16)
    product = lax.dot_general(act_panel.astype(jnp.float32), coeff.astype(jnp.float32), (((1,), (1,)), ((), ())), preferred_element_type=jnp.float32)
    updated = (act_trail.astype(jnp.float32) - product).astype(jnp.bfloat16)
    return (triangle, top_rows, updated)
```

```python
import functools
import jax
import jax.numpy as jnp
from jax import lax
from jax.sharding import PartitionSpec as P
from jax.experimental import pallas as pl
from jax.experimental.pallas import tpu as pltpu

TILE = 128
F32 = jnp.float32
BF16 = jnp.bfloat16
VMEM = pl.BlockSpec(memory_space=pltpu.VMEM)
SMEM = pl.BlockSpec(memory_space=pltpu.SMEM)
ANY = pl.BlockSpec(memory_space=pl.ANY)
MIB = 1 << 20


def shape(dims, kind):
    return jax.ShapeDtypeStruct(dims, kind)


def call(body, name, out_shape, in_specs, out_specs, grant, flops=0, moved=0, scratch=()):
    return pl.pallas_call(
        body,
        name=name,
        out_shape=out_shape,
        in_specs=in_specs,
        out_specs=out_specs,
        scratch_shapes=list(scratch),
        cost_estimate=pl.CostEstimate(flops=flops, bytes_accessed=moved, transcendentals=0),
        compiler_params=pltpu.CompilerParams(vmem_limit_bytes=grant * MIB),
    )


def dot(a, b, contract):
    return lax.dot_general(a, b, (contract, ((), ())), preferred_element_type=F32)


def exact(a, b, contract):
    return lax.dot_general(
        a, b, (contract, ((), ())), precision=lax.Precision.HIGHEST, preferred_element_type=F32
    )


def split(value):
    high = value.astype(BF16)
    return high, (value - high.astype(F32)).astype(BF16)


def pick_kernel(tiles, panel, out):
    for k in range(tiles.shape[0]):
        start = pl.multiple_of(tiles[k] * TILE, TILE)
        block = panel[pl.ds(start, TILE), :].astype(F32)
        out[:, k * TILE : (k + 1) * TILE] = block.T.astype(BF16)


def pick(tile_list, panel):
    rows = tile_list.shape[0] * TILE
    return call(
        pick_kernel, "pick", shape((panel.shape[1], rows), BF16), [SMEM, VMEM], VMEM, 8,
        moved=4 * rows * panel.shape[1],
    )(tile_list, panel)


def gram_kernel(parts, place, *refs):
    blocks, (full, keep, send) = refs[: 2 * parts - 1], refs[2 * parts - 1 :]
    z, core = place[0], place[1]
    wide = blocks[0].shape[0]
    full[pl.ds(pl.multiple_of(z * wide, wide), wide), :] = blocks[0][...]
    for d in range(1, parts):
        @pl.when(z >= d)
        def _(d=d):
            full[pl.ds(pl.multiple_of((z - d) * wide, wide), wide), :] = blocks[2 * d - 1][...]

        @pl.when(z + d < parts)
        def _(d=d):
            full[pl.ds(pl.multiple_of((z + d) * wide, wide), wide), :] = blocks[2 * d][...]

    half = keep.shape[0]
    everything = full[...]
    mine = full[pl.ds(pl.multiple_of(core * half, half), half), :]
    theirs = full[pl.ds(pl.multiple_of((1 - core) * half, half), half), :]
    send[...] = dot(theirs, everything, ((1,), (1,)))
    keep[...] = dot(mine, everything, ((1,), (1,)))


def gram(place, blocks, parts):
    wide, rows = blocks[0].shape
    width = parts * wide
    half = shape((width // 2, width), F32)
    return call(
        functools.partial(gram_kernel, parts), "gram", (shape((width, rows), BF16), half, half),
        [SMEM] + [VMEM] * len(blocks), (VMEM, VMEM, VMEM), 16,
        flops=2 * width * width * rows, moved=4 * width * rows,
    )(place, *blocks)


def turn_kernel(full, out):
    step = 2 * TILE
    for k in range(full.shape[1] // step):
        out[k * step : (k + 1) * step, :] = full[:, k * step : (k + 1) * step].astype(F32).T.astype(BF16)


def turn(full):
    width, rows = full.shape
    return call(turn_kernel, "turn", shape((rows, width), BF16), [VMEM], VMEM, 16, moved=4 * width * rows)(full)


def fetch(tiles, source, buffer, sems, column, slot):
    wide = buffer.shape[2]
    for k in range(tiles.shape[0]):
        start = pl.multiple_of(tiles[k] * TILE, TILE)
        pltpu.make_async_copy(
            source.at[pl.ds(start, TILE), pl.ds(column, wide)],
            buffer.at[slot, pl.ds(k * TILE, TILE), :],
            sems.at[slot],
        ).start()


def arrive(source, buffer, sems, slot):
    rows, wide = buffer.shape[1:]
    pltpu.make_async_copy(source.at[pl.ds(0, rows), pl.ds(0, wide)], buffer.at[slot], sems.at[slot]).wait()


def cross_kernel(prepare, steps, tiles, place, *refs):
    *sources, trailing, keep, send, lhs, buffer, sems = refs
    core = place[1]
    half = keep.shape[1]
    wide = buffer.shape[2]

    def column(i):
        side = jnp.where(i < steps // 2, 1 - core, core)
        return pl.multiple_of(side * half + lax.rem(i, steps // 2) * wide, wide)

    fetch(tiles, trailing, buffer, sems, column(0), 0)
    prepare(place, sources, lhs)

    def body(i, _):
        slot = lax.rem(i, 2)

        @pl.when(i + 1 < steps)
        def _():
            fetch(tiles, trailing, buffer, sems, column(i + 1), 1 - slot)

        arrive(trailing, buffer, sems, slot)
        value = dot(lhs[...], buffer[slot], ((1,), (0,)))
        where = pl.ds(pl.multiple_of(lax.rem(i, steps // 2) * wide, wide), wide)

        @pl.when(i < steps // 2)
        def _():
            send[:, where] = value.astype(BF16)

        @pl.when(i >= steps // 2)
        def _():
            keep[:, where] = value

        return 0

    lax.fori_loop(0, steps, body, 0)


def cross(name, prepare, deep, tile_list, place, sources, trailing):
    rows = tile_list.shape[0] * TILE
    columns = trailing.shape[1]
    steps = 8
    wide = columns // steps
    return call(
        functools.partial(cross_kernel, prepare, steps), name,
        (shape((deep, columns // 2), F32), shape((deep, columns // 2), BF16)),
        [SMEM, SMEM] + [VMEM] * len(sources) + [ANY], (VMEM, VMEM), 24,
        flops=2 * deep * rows * columns, moved=2 * rows * columns,
        scratch=(
            pltpu.VMEM((deep, rows), BF16),
            pltpu.VMEM((2, rows, wide), BF16),
            pltpu.SemaphoreType.DMA((2,)),
        ),
    )(tile_list, place, *sources, trailing)


def pair_lhs(place, sources, lhs):
    own, below, above = sources
    wide = own.shape[0]

    @pl.when(lax.rem(place[0], 2) == 0)
    def _():
        lhs[:wide, :] = own[...]
        lhs[wide:, :] = above[...]

    @pl.when(lax.rem(place[0], 2) == 1)
    def _():
        lhs[:wide, :] = below[...]
        lhs[wide:, :] = own[...]


def other_lhs(place, sources, lhs):
    (full,) = sources
    pair = lax.div(place[0], 2)
    wide = full.shape[0] - lhs.shape[0]
    for k in range(lhs.shape[0] // wide):
        q = k + (k >= pair).astype(jnp.int32)
        lhs[k * wide : (k + 1) * wide, :] = full[pl.ds(pl.multiple_of(q * wide, wide), wide), :]


def share_kernel(place, keep, got, own, *outs):
    chip = place[2]
    wide = own.shape[1]

    def total(where):
        return keep[:, where] + got[:, where].astype(F32)

    own[...] = total(pl.ds(pl.multiple_of(chip * wide, wide), wide))
    for s, out in enumerate(outs, 1):
        out[...] = total(pl.ds(pl.multiple_of((chip ^ s) * wide, wide), wide)).astype(BF16)


def share(place, keep, got, chips):
    deep, columns = keep.shape
    wide = columns // chips
    return call(
        share_kernel, "share", [shape((deep, wide), F32)] + [shape((deep, wide), BF16)] * (chips - 1),
        [SMEM, VMEM, VMEM], [VMEM] * chips, 8, moved=8 * deep * columns,
    )(place, keep, got)


def swap(value, bit, rows):
    return lax.ppermute(value, "row", [(i, i ^ bit) for i in range(rows)])


def tree(values):
    values = [v.astype(F32) for v in values]
    while len(values) > 1:
        values = [a + b for a, b in zip(values[::2], values[1::2])]
    return values[0]


def reduce_cross(place, keep, send, rows):
    chips = rows // 2
    got = swap(send, 1, rows)
    own, *outs = share(place, keep, got, chips)
    parts = [own] + [swap(v, 2 * s, rows) for s, v in enumerate(outs, 1)]
    mine = tree(parts).astype(BF16)
    stack = jnp.stack([mine] + [swap(mine, 2 * s, rows) for s in range(1, chips)])
    return stack, swap(stack, 1, rows)


def reduce_gram(keep, send, rows):
    own = keep + swap(send, 1, rows)
    total = tree([own] + [swap(own, 2 * s, rows) for s in range(1, rows // 2)])
    return total, swap(total, 1, rows)


def eliminate(tiles, size):
    sub = lax.broadcasted_iota(jnp.int32, (8, 1), 0)
    done = []
    for t in range(size // 8):
        for r in range(8):
            j = t * 8 + r
            row = tiles[t][r : r + 1, :]
            scale = lax.rsqrt(row[:, j : j + 1])
            pivot = row * scale
            done.append(pivot)
            for q in range(t, size // 8):
                lead = tiles[q][:, j : j + 1] * scale
                if q == t:
                    lead = jnp.where(sub > r, lead, 0.0)
                tiles[q] = tiles[q] - lead * pivot
    return jnp.concatenate(done, 0)


def factor_kernel(place, mine, theirs, triangle, inverse, turned, whole):
    core = place[1]
    h = mine.shape[0]
    whole[pl.ds(pl.multiple_of(core * h, h), h), :] = mine[...]
    whole[pl.ds(pl.multiple_of((1 - core) * h, h), h), :] = theirs[...]
    line = lax.broadcasted_iota(jnp.int32, (h, h), 0)
    lane = lax.broadcasted_iota(jnp.int32, (h, h), 1)
    eye = (line == lane).astype(F32)
    zero = jnp.zeros((h, h), F32)
    first = jnp.concatenate([whole[:h, :], eye], 1)
    first = eliminate([first[8 * t : 8 * t + 8] for t in range(h // 8)], h)
    r11, r12, i11 = first[:, :h], first[:, h : 2 * h], first[:, 2 * h :]
    second = jnp.concatenate([whole[h:, h:] - exact(r12, r12, ((0,), (0,))), eye], 1)
    second = eliminate([second[8 * t : 8 * t + 8] for t in range(h // 8)], h)
    r22, i22 = second[:, :h], second[:, h:]
    i11 = jnp.where(lane <= line, i11, 0.0)
    i22 = jnp.where(lane <= line, i22, 0.0)
    i21 = -exact(i22, exact(r12, i11, ((0,), (0,))), ((1,), (0,)))
    triangle[:h, :h] = jnp.where(lane >= line, r11, 0.0)
    triangle[:h, h:] = r12
    triangle[h:, :h] = zero
    triangle[h:, h:] = jnp.where(lane >= line, r22, 0.0)
    full = jnp.concatenate([jnp.concatenate([i11, zero], 1), jnp.concatenate([i21, i22], 1)], 0)
    inverse[0], inverse[1] = split(full)
    turned[0], turned[1] = split(full.T)


def factor(place, mine, theirs):
    size = mine.shape[1]
    both = shape((2, size, size), BF16)
    return call(
        factor_kernel, "factor", (shape((size, size), F32), both, both), [SMEM, VMEM, VMEM], (VMEM,) * 3, 16,
        flops=10 * size**3, moved=30 * MIB, scratch=(pltpu.VMEM((size, size), F32),),
    )(place, mine, theirs)


def update_kernel(
    chips, tiles, place, inverse, turned, panel, near_one, far_one, near_two, far_two, trailing,
    top_out, out, cross_buf, tops, buffer, results, in_sems, top_sems, out_sems,
):
    z, core, chip = place[0], place[1], place[2]
    pair = lax.div(z, 2)
    wide = buffer.shape[2]
    steps = 2 * chips
    two = near_one.shape[1]
    rest = near_two.shape[1] // two
    rows = buffer.shape[1]
    block = 2 * TILE

    def column(i):
        side = jnp.where(i < chips, core, 1 - core)
        return pl.multiple_of((side * chips + (chip ^ lax.rem(i, chips))) * wide, wide)

    fetch(tiles, trailing, buffer, in_sems, column(0), 0)

    def top_copy(slot, where):
        return pltpu.make_async_copy(tops.at[slot], top_out.at[pl.ds(where, wide), :], top_sems.at[slot])

    def out_copy(slot, where):
        return pltpu.make_async_copy(results.at[slot], out.at[:, pl.ds(where, wide)], out_sems.at[slot])

    def body(i, _):
        slot = lax.rem(i, 2)
        where = column(i)
        s = lax.rem(i, chips)

        @pl.when(i + 1 < steps)
        def _():
            fetch(tiles, trailing, buffer, in_sems, column(i + 1), 1 - slot)

        def place_cross(one, several):
            cross_buf[pl.ds(pl.multiple_of(pair * two, two), two), :] = one[s]
            for k in range(rest):
                q = k + (k >= pair).astype(jnp.int32)
                cross_buf[pl.ds(pl.multiple_of(q * two, two), two), :] = several[s, k * two : (k + 1) * two, :]

        @pl.when(i < chips)
        def _():
            place_cross(near_one, near_two)

        @pl.when(i >= chips)
        def _():
            place_cross(far_one, far_two)

        sums = cross_buf[...]
        turn_ = ((1,), (0,))
        top = dot(inverse[0], sums, turn_) + dot(inverse[1], sums, turn_)
        high, low = split(top)
        coeff = (dot(turned[0], high, turn_) + (dot(turned[0], low, turn_) + dot(turned[1], high, turn_))).astype(BF16)

        @pl.when(i >= 2)
        def _():
            top_copy(slot, 0).wait()
            out_copy(slot, 0).wait()

        tops[slot] = top.T
        top_copy(slot, where).start()
        arrive(trailing, buffer, in_sems, slot)

        def rows_body(k, _):
            part = pl.ds(pl.multiple_of(k * block, block), block)
            product = dot(panel[part, :], coeff, turn_)
            results[slot, part, :] = (buffer[slot, part, :].astype(F32) - product).astype(BF16)
            return 0

        lax.fori_loop(0, rows // block, rows_body, 0, unroll=True)
        out_copy(slot, where).start()
        return 0

    lax.fori_loop(0, steps, body, 0)
    for slot in range(2):
        top_copy(slot, 0).wait()
        out_copy(slot, 0).wait()


def update(tile_list, place, inverse, turned, panel, one, two, trailing, chips):
    rows, size = panel.shape
    columns = trailing.shape[1]
    wide = columns // (2 * chips)
    return call(
        functools.partial(update_kernel, chips), "update",
        (shape((columns, size), F32), shape((rows, columns), BF16)),
        [SMEM, SMEM] + [VMEM] * 7 + [ANY], (ANY, ANY), 40,
        flops=2 * rows * size * columns, moved=4 * rows * columns,
        scratch=(
            pltpu.VMEM((size, wide), BF16),
            pltpu.VMEM((2, wide, size), F32),
            pltpu.VMEM((2, rows, wide), BF16),
            pltpu.VMEM((2, rows, wide), BF16),
            pltpu.SemaphoreType.DMA((2,)),
            pltpu.SemaphoreType.DMA((2,)),
            pltpu.SemaphoreType.DMA((2,)),
        ),
    )(tile_list, place, inverse, turned, panel, *one, *two, trailing)


def local(nrow, ncol, panel, trailing, tile_list):
    row = lax.axis_index("row")
    place = jnp.stack([lax.axis_index("col"), row % 2, row // 2]).astype(jnp.int32)
    own = pick(tile_list, panel)
    below, above = [own], [own]
    for s in range(1, ncol):
        below.append(lax.ppermute(below[-1], "col", [(i, i + 1) for i in range(s - 1, ncol - 1)]))
        above.append(lax.ppermute(above[-1], "col", [(i + 1, i) for i in range(ncol - s)]))
    wide = panel.shape[1]
    one = cross("cross_pair", pair_lhs, 2 * wide, tile_list, place, [own, below[1], above[1]], trailing)
    one = reduce_cross(place, *one, nrow)
    blocks = [own]
    for s in range(1, ncol):
        blocks += [below[s], above[s]]
    full, keep, send = gram(place, blocks, ncol)
    sums = reduce_gram(keep, send, nrow)
    two = cross("cross_rest", other_lhs, (ncol - 2) * wide, tile_list, place, [full], trailing)
    two = reduce_cross(place, *two, nrow)
    triangle, inverse, turned = factor(place, *sums)
    top_rows, updated = update(
        tile_list, place, inverse, turned, turn(full), one, two, trailing, nrow // 2
    )
    return triangle, top_rows, updated


def solution(mesh):
    return jax.shard_map(
        functools.partial(local, mesh.shape["row"], mesh.shape["col"]),
        mesh=mesh,
        in_specs=(P("row", "col"), P("row", "col"), P("row")),
        out_specs=(P(), P("col", None), P("row", "col")),
        check_vma=False,
    )
```

```python
import functools
import jax
import jax.numpy as jnp
from jax import lax
from jax.sharding import PartitionSpec as P
from jax.experimental import pallas as pl
from jax.experimental.pallas import tpu as pltpu

TILE = 128
F32 = jnp.float32
BF16 = jnp.bfloat16
VMEM = pl.BlockSpec(memory_space=pltpu.VMEM)
SMEM = pl.BlockSpec(memory_space=pltpu.SMEM)
ANY = pl.BlockSpec(memory_space=pl.ANY)
MIB = 1 << 20


def shape(dims, kind):
    return jax.ShapeDtypeStruct(dims, kind)


def call(body, out_shape, in_specs, out_specs, grant, flops=0, moved=0, scratch=()):
    return pl.pallas_call(
        body,
        out_shape=out_shape,
        in_specs=in_specs,
        out_specs=out_specs,
        scratch_shapes=list(scratch),
        cost_estimate=pl.CostEstimate(flops=flops, bytes_accessed=moved, transcendentals=0),
        compiler_params=pltpu.CompilerParams(vmem_limit_bytes=grant * MIB),
    )


def dot(a, b, contract):
    return lax.dot_general(a, b, (contract, ((), ())), preferred_element_type=F32)


def exact(a, b, contract):
    return lax.dot_general(
        a, b, (contract, ((), ())), precision=lax.Precision.HIGHEST, preferred_element_type=F32
    )


def split(value):
    high = value.astype(BF16)
    return high, (value - high.astype(F32)).astype(BF16)


def pick_kernel(tiles, panel, out):
    for k in range(tiles.shape[0]):
        start = pl.multiple_of(tiles[k] * TILE, TILE)
        out[:, k * TILE : (k + 1) * TILE] = panel[:, pl.ds(start, TILE)]


def pick(tile_list, panel):
    rows = tile_list.shape[0] * TILE
    return call(
        pick_kernel, shape((panel.shape[0], rows), BF16), [SMEM, VMEM], VMEM, 8,
        moved=4 * rows * panel.shape[0],
    )(tile_list, panel)


def gram_kernel(place, *refs):
    *blocks, full, keep, send = refs
    z, core = place[0], place[1]
    wide = blocks[0].shape[0]
    for s, block in enumerate(blocks):
        full[pl.ds(pl.multiple_of((z ^ s) * wide, wide), wide), :] = block[...]
    half = keep.shape[0]
    everything = full[...]
    mine = full[pl.ds(pl.multiple_of(core * half, half), half), :]
    theirs = full[pl.ds(pl.multiple_of((1 - core) * half, half), half), :]
    send[...] = dot(theirs, everything, ((1,), (1,)))
    keep[...] = dot(mine, everything, ((1,), (1,)))


def gram(place, blocks):
    wide, rows = blocks[0].shape
    width = len(blocks) * wide
    half = shape((width // 2, width), F32)
    return call(
        gram_kernel, (shape((width, rows), BF16), half, half),
        [SMEM] + [VMEM] * len(blocks), (VMEM, VMEM, VMEM), 16,
        flops=2 * width * width * rows, moved=4 * width * rows,
    )(place, *blocks)


def turn_kernel(full, out):
    step = 2 * TILE
    for k in range(full.shape[1] // step):
        out[k * step : (k + 1) * step, :] = full[:, k * step : (k + 1) * step].astype(F32).T.astype(BF16)


def turn(full):
    width, rows = full.shape
    return call(turn_kernel, shape((rows, width), BF16), [VMEM], VMEM, 16, moved=4 * width * rows)(full)


def cross_pair_kernel(steps, tiles, place, own, other, trailing, active, keep, send, lhs, sems):
    core, odd = place[1], lax.rem(place[0], 2)
    half = keep.shape[1]
    wide = active.shape[1] // steps
    deep = own.shape[0]

    def column(i):
        side = jnp.where(i < steps // 2, 1 - core, core)
        return pl.multiple_of(side * half + lax.rem(i, steps // 2) * wide, wide)

    def issue(i, _):
        for k in range(tiles.shape[0]):
            start = pl.multiple_of(tiles[k] * TILE, TILE)
            where = pl.ds(column(i), wide)
            pltpu.make_async_copy(
                trailing.at[pl.ds(start, TILE), where], active.at[pl.ds(k * TILE, TILE), where], sems.at[i]
            ).start()
        return 0

    lax.fori_loop(0, steps, issue, 0)
    lhs[pl.ds(pl.multiple_of(odd * deep, deep), deep), :] = own[...]
    lhs[pl.ds(pl.multiple_of((1 - odd) * deep, deep), deep), :] = other[...]

    def body(i, _):
        source = pl.ds(column(i), wide)
        rows = active.shape[0]
        pltpu.make_async_copy(trailing.at[pl.ds(0, rows), source], active.at[:, source], sems.at[i]).wait()
        value = dot(lhs[...], active[:, source], ((1,), (0,)))
        where = pl.ds(pl.multiple_of(lax.rem(i, steps // 2) * wide, wide), wide)

        @pl.when(i < steps // 2)
        def _():
            send[:, where] = value.astype(BF16)

        @pl.when(i >= steps // 2)
        def _():
            keep[:, where] = value

        return 0

    lax.fori_loop(0, steps, body, 0)


def cross_pair(tile_list, place, own, other, trailing):
    deep, rows = own.shape
    columns = trailing.shape[1]
    steps = 8
    return call(
        functools.partial(cross_pair_kernel, steps),
        (pltpu.VMEM((rows, columns), BF16), shape((2 * deep, columns // 2), F32), shape((2 * deep, columns // 2), BF16)),
        [SMEM, SMEM, VMEM, VMEM, ANY], (VMEM,) * 3, 8,
        flops=4 * deep * rows * columns, moved=2 * rows * columns,
        scratch=(pltpu.VMEM((2 * deep, rows), BF16), pltpu.SemaphoreType.DMA((steps,))),
    )(tile_list, place, own, other, trailing)


def cross_rest_kernel(steps, mine, place, full, active, out, lhs):
    pair = lax.div(place[0], 2)
    side = place[1] if mine else 1 - place[1]
    across = full.shape[0] - lhs.shape[0]
    wide = out.shape[1] // steps
    for k in range(lhs.shape[0] // across):
        q = k + (k >= pair).astype(jnp.int32)
        lhs[k * across : (k + 1) * across, :] = full[pl.ds(pl.multiple_of(q * across, across), across), :]

    def body(i, _):
        source = pl.ds(pl.multiple_of(side * out.shape[1] + i * wide, wide), wide)
        where = pl.ds(pl.multiple_of(i * wide, wide), wide)
        out[:, where] = dot(lhs[...], active[:, source], ((1,), (0,))).astype(out.dtype)
        return 0

    lax.fori_loop(0, steps, body, 0)


def cross_rest(mine, place, full, active, across):
    deep = full.shape[0] - across
    rows, columns = active.shape
    return call(
        functools.partial(cross_rest_kernel, 4, mine),
        shape((deep, columns // 2), F32 if mine else BF16), [SMEM, VMEM, VMEM], VMEM, 8,
        flops=deep * rows * columns, moved=rows * columns,
        scratch=(pltpu.VMEM((deep, rows), BF16),),
    )(place, full, active)


def share_kernel(place, keep, got, own, *outs):
    chip = place[2]
    wide = own.shape[1]

    def total(where):
        return keep[:, where] + got[:, where].astype(F32)

    own[...] = total(pl.ds(pl.multiple_of(chip * wide, wide), wide))
    for s, out in enumerate(outs, 1):
        out[...] = total(pl.ds(pl.multiple_of((chip ^ s) * wide, wide), wide)).astype(BF16)


def share(place, keep, got, chips):
    deep, columns = keep.shape
    wide = columns // chips
    return call(
        share_kernel, [shape((deep, wide), F32)] + [shape((deep, wide), BF16)] * (chips - 1),
        [SMEM, VMEM, VMEM], [VMEM] * chips, 8, moved=8 * deep * columns,
    )(place, keep, got)


def swap(value, bit, rows):
    return lax.ppermute(value, "row", [(i, i ^ bit) for i in range(rows)])


def tree(values):
    values = [v.astype(F32) for v in values]
    while len(values) > 1:
        values = [a + b for a, b in zip(values[::2], values[1::2])]
    return values[0]


def reduce_cross(place, keep, got, rows):
    chips = rows // 2
    own, *outs = share(place, keep, got, chips)
    parts = [own] + [swap(v, 2 * s, rows) for s, v in enumerate(outs, 1)]
    mine = tree(parts).astype(BF16)
    stack = jnp.stack([mine] + [swap(mine, 2 * s, rows) for s in range(1, chips)])
    return stack, swap(stack, 1, rows)


def reduce_gram(keep, send, rows):
    own = keep + swap(send, 1, rows)
    total = tree([own] + [swap(own, 2 * s, rows) for s in range(1, rows // 2)])
    return total, swap(total, 1, rows)


def eliminate(tiles, size):
    sub = lax.broadcasted_iota(jnp.int32, (8, 1), 0)
    done = []
    for t in range(size // 8):
        for r in range(8):
            j = t * 8 + r
            row = tiles[t][r : r + 1, :]
            scale = lax.rsqrt(row[:, j : j + 1])
            pivot = row * scale
            done.append(pivot)
            for q in range(t, size // 8):
                lead = tiles[q][:, j : j + 1] * scale
                if q == t:
                    lead = jnp.where(sub > r, lead, 0.0)
                tiles[q] = tiles[q] - lead * pivot
    return jnp.concatenate(done, 0)


def rows_of(value):
    return [value[8 * t : 8 * t + 8] for t in range(value.shape[0] // 8)]


def factor_first_kernel(place, mine, theirs, first, rest, whole):
    core = place[1]
    h = mine.shape[0]
    whole[pl.ds(pl.multiple_of(core * h, h), h), :] = mine[...]
    whole[pl.ds(pl.multiple_of((1 - core) * h, h), h), :] = theirs[...]
    line = lax.broadcasted_iota(jnp.int32, (h, h), 0)
    lane = lax.broadcasted_iota(jnp.int32, (h, h), 1)
    eye = (line == lane).astype(F32)
    value = eliminate(rows_of(jnp.concatenate([whole[:h, :], eye], 1)), h)
    first[...] = value
    r12 = value[:, h : 2 * h]
    rest[...] = whole[h:, h:] - exact(r12, r12, ((0,), (0,)))


def factor_last_kernel(first, rest, triangle, inverse, turned):
    h = first.shape[0]
    line = lax.broadcasted_iota(jnp.int32, (h, h), 0)
    lane = lax.broadcasted_iota(jnp.int32, (h, h), 1)
    eye = (line == lane).astype(F32)
    zero = jnp.zeros((h, h), F32)
    second = eliminate(rows_of(jnp.concatenate([rest[...], eye], 1)), h)
    r11, r12, i11 = first[:, :h], first[:, h : 2 * h], first[:, 2 * h :]
    r22, i22 = second[:, :h], second[:, h:]
    i11 = jnp.where(lane <= line, i11, 0.0)
    i22 = jnp.where(lane <= line, i22, 0.0)
    i21 = -exact(i22, exact(r12, i11, ((0,), (0,))), ((1,), (0,)))
    triangle[:h, :h] = jnp.where(lane >= line, r11, 0.0)
    triangle[:h, h:] = r12
    triangle[h:, :h] = zero
    triangle[h:, h:] = jnp.where(lane >= line, r22, 0.0)
    full = jnp.concatenate([jnp.concatenate([i11, zero], 1), jnp.concatenate([i21, i22], 1)], 0)
    inverse[0], inverse[1] = split(full)
    turned[0], turned[1] = split(full.T)


def factor_first(place, mine, theirs):
    h, size = mine.shape
    return call(
        factor_first_kernel, (shape((h, 3 * h), F32), shape((h, h), F32)), [SMEM, VMEM, VMEM],
        (VMEM,) * 2, 8, flops=10 * size**3, moved=20 * MIB, scratch=(pltpu.VMEM((size, size), F32),),
    )(place, mine, theirs)


def factor_last(first, rest):
    size = 2 * first.shape[0]
    both = shape((2, size, size), BF16)
    return call(
        factor_last_kernel, (shape((size, size), F32), both, both), [VMEM, VMEM], (VMEM,) * 3, 8,
        flops=10 * size**3, moved=20 * MIB,
    )(first, rest)


def update_kernel(
    chips, place, inverse, turned, panel, near_one, far_one, near_two, far_two, active,
    top_out, out, cross_buf, tops, results, top_sems, out_sems,
):
    z, core, chip = place[0], place[1], place[2]
    pair = lax.div(z, 2)
    wide = results.shape[2]
    steps = 2 * chips
    two = near_one.shape[1]
    rest = near_two.shape[1] // two
    rows = results.shape[1]
    block = 2 * TILE

    def column(i):
        side = jnp.where(i < chips, core, 1 - core)
        return pl.multiple_of((side * chips + (chip ^ lax.rem(i, chips))) * wide, wide)

    def top_copy(slot, where):
        return pltpu.make_async_copy(tops.at[slot], top_out.at[pl.ds(where, wide), :], top_sems.at[slot])

    def out_copy(slot, where):
        return pltpu.make_async_copy(results.at[slot], out.at[:, pl.ds(where, wide)], out_sems.at[slot])

    def body(i, _):
        slot = lax.rem(i, 2)
        where = column(i)
        s = lax.rem(i, chips)

        def place_cross(one, several):
            cross_buf[pl.ds(pl.multiple_of(pair * two, two), two), :] = one[s]
            for k in range(rest):
                q = k + (k >= pair).astype(jnp.int32)
                cross_buf[pl.ds(pl.multiple_of(q * two, two), two), :] = several[s, k * two : (k + 1) * two, :]

        @pl.when(i < chips)
        def _():
            place_cross(near_one, near_two)

        @pl.when(i >= chips)
        def _():
            place_cross(far_one, far_two)

        sums = cross_buf[...]
        turn_ = ((1,), (0,))
        top = dot(inverse[0], sums, turn_) + dot(inverse[1], sums, turn_)
        high, low = split(top)
        coeff = (dot(turned[0], high, turn_) + (dot(turned[0], low, turn_) + dot(turned[1], high, turn_))).astype(BF16)

        @pl.when(i >= 2)
        def _():
            top_copy(slot, 0).wait()
            out_copy(slot, 0).wait()

        tops[slot] = top.T
        top_copy(slot, where).start()

        def rows_body(k, _):
            part = pl.ds(pl.multiple_of(k * block, block), block)
            product = dot(panel[part, :], coeff, turn_)
            results[slot, part, :] = (active[part, pl.ds(where, wide)].astype(F32) - product).astype(BF16)
            return 0

        lax.fori_loop(0, rows // block, rows_body, 0, unroll=True)
        out_copy(slot, where).start()
        return 0

    lax.fori_loop(0, steps, body, 0)
    for slot in range(2):
        top_copy(slot, 0).wait()
        out_copy(slot, 0).wait()


def update(place, inverse, turned, panel, one, two, active, chips):
    rows, size = panel.shape
    columns = active.shape[1]
    wide = columns // (2 * chips)
    return call(
        functools.partial(update_kernel, chips),
        (shape((columns, size), F32), shape((rows, columns), BF16)),
        [SMEM] + [VMEM] * 8, (ANY, ANY), 12,
        flops=2 * rows * size * columns, moved=2 * rows * columns,
        scratch=(
            pltpu.VMEM((size, wide), BF16),
            pltpu.VMEM((2, wide, size), F32),
            pltpu.VMEM((2, rows, wide), BF16),
            pltpu.SemaphoreType.DMA((2,)),
            pltpu.SemaphoreType.DMA((2,)),
        ),
    )(place, inverse, turned, panel, *one, *two, active)


def local(nrow, ncol, panel, trailing, tile_list):
    row = lax.axis_index("row")
    place = jnp.stack([lax.axis_index("col"), row % 2, row // 2]).astype(jnp.int32)
    own = pick(tile_list, panel.T)
    blocks = [own]
    for s in range(1, ncol):
        blocks.append(lax.ppermute(own, "col", [(i, i ^ s) for i in range(ncol)]))
    across = 2 * panel.shape[1]
    active, keep, send = cross_pair(tile_list, place, own, blocks[1], trailing)
    one = reduce_cross(place, keep, swap(send, 1, nrow), nrow)
    full, keep, send = gram(place, blocks)
    sums = reduce_gram(keep, send, nrow)
    turned_panel = turn(full)
    send = cross_rest(False, place, full, active, across)
    send = swap(send, 1, nrow)
    keep = cross_rest(True, place, full, active, across)
    two = reduce_cross(place, keep, send, nrow)
    triangle, inverse, turned = factor_last(*factor_first(place, *sums))
    top_rows, updated = update(place, inverse, turned, turned_panel, one, two, active, nrow // 2)
    return triangle, top_rows, updated


def solution(mesh):
    nrow, ncol = mesh.shape["row"], mesh.shape["col"]

    def program(panel, trailing, tile_list):
        return local(nrow, ncol, panel, trailing, tile_list)

    return jax.shard_map(
        program,
        mesh=mesh,
        in_specs=(P("row", "col"), P("row", "col"), P("row")),
        out_specs=(P(), P("col", None), P("row", "col")),
        check_vma=False,
    )
```

```python
import functools
import jax
import jax.numpy as jnp
from jax import lax
from jax.sharding import PartitionSpec as P
from jax.experimental import pallas as pl
from jax.experimental.pallas import tpu as pltpu

TILE = 128
BAND = 4
F32 = jnp.float32
BF16 = jnp.bfloat16
VMEM = pl.BlockSpec(memory_space=pltpu.VMEM)
SMEM = pl.BlockSpec(memory_space=pltpu.SMEM)
ANY = pl.BlockSpec(memory_space=pl.ANY)
HBM = pl.BlockSpec(memory_space=pltpu.HBM)
MIB = 1 << 20


def shape(dims, kind):
    return jax.ShapeDtypeStruct(dims, kind)


def call(body, out_shape, in_specs, out_specs, grant, flops=0, moved=0, scratch=()):
    return pl.pallas_call(
        body,
        out_shape=out_shape,
        in_specs=in_specs,
        out_specs=out_specs,
        scratch_shapes=list(scratch),
        cost_estimate=pl.CostEstimate(flops=flops, bytes_accessed=moved, transcendentals=0),
        compiler_params=pltpu.CompilerParams(vmem_limit_bytes=grant * MIB),
    )


def stay(value):
    return pltpu.with_memory_space_constraint(value, pltpu.HBM)


def dot(a, b, contract):
    return lax.dot_general(a, b, (contract, ((), ())), preferred_element_type=F32)


def exact(a, b, contract):
    return lax.dot_general(
        a, b, (contract, ((), ())), precision=lax.Precision.HIGHEST, preferred_element_type=F32
    )


def split(value):
    high = value.astype(BF16)
    return high, (value - high.astype(F32)).astype(BF16)


def pick_kernel(listed, source, out, tiles, panel, sems):
    copies = (
        pltpu.make_async_copy(listed, tiles, sems.at[0]),
        pltpu.make_async_copy(source, panel, sems.at[1]),
    )
    for copy in copies:
        copy.start()
    for copy in copies:
        copy.wait()
    for k in range(tiles.shape[0]):
        start = pl.multiple_of(tiles[k] * TILE, TILE)
        out[:, k * TILE : (k + 1) * TILE] = panel[:, pl.ds(start, TILE)]


def pick(tile_list, panel):
    rows = tile_list.shape[0] * TILE
    return call(
        pick_kernel, shape((panel.shape[0], rows), BF16), [HBM, HBM], VMEM, 8,
        moved=4 * rows * panel.shape[0],
        scratch=(
            pltpu.SMEM(tile_list.shape, jnp.int32),
            pltpu.VMEM(panel.shape, BF16),
            pltpu.SemaphoreType.DMA((2,)),
        ),
    )(stay(tile_list), stay(panel))


def load_kernel(listed, trailing, active, tiles, sems):
    copy = pltpu.make_async_copy(listed, tiles, sems.at[0])
    copy.start()
    copy.wait()
    for k in range(tiles.shape[0]):
        start = pl.multiple_of(tiles[k] * TILE, TILE)
        pltpu.make_async_copy(
            trailing.at[pl.ds(start, TILE), :], active.at[pl.ds(k * TILE, TILE), :], sems.at[1]
        ).start()
    pltpu.make_async_copy(trailing.at[pl.ds(0, active.shape[0]), :], active, sems.at[1]).wait()


def load(tile_list, trailing):
    rows = tile_list.shape[0] * TILE
    columns = trailing.shape[1]
    return call(
        load_kernel, pltpu.VMEM((rows, columns), BF16), [HBM, HBM], VMEM, 8,
        moved=2 * rows * columns,
        scratch=(pltpu.SMEM(tile_list.shape, jnp.int32), pltpu.SemaphoreType.DMA((2,))),
    )(stay(tile_list), trailing)


def gram_kernel(place, *refs):
    *blocks, full, keep, send = refs
    z, core = place[0], place[1]
    wide = blocks[0].shape[0]
    for s, block in enumerate(blocks):
        full[pl.ds(pl.multiple_of((z ^ s) * wide, wide), wide), :] = block[...]
    half = keep.shape[0]
    everything = full[...]
    mine = full[pl.ds(pl.multiple_of(core * half, half), half), :]
    theirs = full[pl.ds(pl.multiple_of((1 - core) * half, half), half), :]
    send[...] = dot(theirs, everything, ((1,), (1,)))
    keep[...] = dot(mine, everything, ((1,), (1,)))


def gram(place, blocks):
    wide, rows = blocks[0].shape
    width = len(blocks) * wide
    half = shape((width // 2, width), F32)
    return call(
        gram_kernel, (shape((width, rows), BF16), half, half),
        [SMEM] + [VMEM] * len(blocks), (VMEM, VMEM, VMEM), 16,
        flops=2 * width * width * rows, moved=4 * width * rows,
    )(place, *blocks)


def turn_kernel(full, out):
    step = 2 * TILE
    for k in range(full.shape[1] // step):
        out[k * step : (k + 1) * step, :] = full[:, k * step : (k + 1) * step].astype(F32).T.astype(BF16)


def turn(full):
    width, rows = full.shape
    return call(turn_kernel, shape((rows, width), BF16), [VMEM], VMEM, 16, moved=4 * width * rows)(full)


def pair_lhs(place, sources, lhs):
    odd = lax.rem(place[0], 2)
    for k, source in enumerate(sources):
        deep = source.shape[0]
        lhs[pl.ds(pl.multiple_of((odd ^ k) * deep, deep), deep), :] = source[...]


def rest_lhs(place, sources, lhs):
    (full,) = sources
    pair = lax.div(place[0], 2)
    across = full.shape[0] - lhs.shape[0]
    for k in range(lhs.shape[0] // across):
        q = k + (k >= pair).astype(jnp.int32)
        lhs[k * across : (k + 1) * across, :] = full[pl.ds(pl.multiple_of(q * across, across), across), :]


def cross_kernel(prepare, steps, mine, place, *refs):
    *sources, active, out, lhs = refs
    side = place[1] if mine else 1 - place[1]
    wide = out.shape[1] // steps
    prepare(place, sources, lhs)

    def body(i, _):
        source = pl.ds(pl.multiple_of(side * out.shape[1] + i * wide, wide), wide)
        where = pl.ds(pl.multiple_of(i * wide, wide), wide)
        out[:, where] = dot(lhs[...], active[:, source], ((1,), (0,))).astype(out.dtype)
        return 0

    lax.fori_loop(0, steps, body, 0)


def cross(prepare, mine, deep, place, sources, active):
    rows, columns = active.shape
    return call(
        functools.partial(cross_kernel, prepare, 4, mine),
        shape((deep, columns // 2), F32 if mine else BF16), [SMEM] + [VMEM] * (len(sources) + 1), VMEM, 8,
        flops=deep * rows * columns, moved=rows * columns,
        scratch=(pltpu.VMEM((deep, rows), BF16),),
    )(place, *sources, active)


def share_kernel(place, keep, got, own, *outs):
    chip = place[2]
    wide = own.shape[1]

    def total(where):
        return keep[:, where] + got[:, where].astype(F32)

    own[...] = total(pl.ds(pl.multiple_of(chip * wide, wide), wide))
    for s, out in enumerate(outs, 1):
        out[...] = total(pl.ds(pl.multiple_of((chip ^ s) * wide, wide), wide)).astype(BF16)


def share(place, keep, got, chips):
    deep, columns = keep.shape
    wide = columns // chips
    return call(
        share_kernel, [shape((deep, wide), F32)] + [shape((deep, wide), BF16)] * (chips - 1),
        [SMEM, VMEM, VMEM], [VMEM] * chips, 8, moved=8 * deep * columns,
    )(place, keep, got)


def swap(value, bit, rows):
    return lax.ppermute(value, "row", [(i, i ^ bit) for i in range(rows)])


def tree(values):
    values = [v.astype(F32) for v in values]
    while len(values) > 1:
        values = [a + b for a, b in zip(values[::2], values[1::2])]
    return values[0]


def reduce_cross(place, keep, got, rows):
    chips = rows // 2
    own, *outs = share(place, keep, got, chips)
    parts = [own] + [swap(v, 2 * s, rows) for s, v in enumerate(outs, 1)]
    mine = tree(parts).astype(BF16)
    stack = jnp.stack([mine] + [swap(mine, 2 * s, rows) for s in range(1, chips)])
    return stack, swap(stack, 1, rows)


def reduce_gram(keep, send, rows):
    own = keep + swap(send, 1, rows)
    total = tree([own] + [swap(own, 2 * s, rows) for s in range(1, rows // 2)])
    return total, swap(total, 1, rows)


def spread(value, r):
    return jnp.broadcast_to(value[r : r + 1, :], (8, 128))


def eliminate(value, size):
    sub = lax.broadcasted_iota(jnp.int32, (8, 128), 0)
    lanes = range(value.shape[1] // 128)
    count = size // 8
    span = min(BAND, count)
    x = [[value[8 * q : 8 * q + 8, 128 * n : 128 * n + 128] for n in lanes] for q in range(count)]
    done = []
    for begin in range(0, count, span):
        end = begin + span
        band = []
        for t in range(begin, end):
            group, at = divmod(8 * t, 128)
            lead = [
                [jnp.broadcast_to(x[q][group][:, at + c : at + c + 1], (8, 128)) for c in range(8)]
                for q in range(t, end)
            ]
            out = [jnp.zeros((8, 128), F32) for _ in lanes]
            for r in range(8):
                root = lax.rsqrt(spread(lead[0][r], r))
                inverse = root * root
                rows = [spread(x[t][n], r) for n in lanes]
                out = [jnp.where(sub == r, v * root, o) for v, o in zip(rows, out)]
                rows = [v * inverse for v in rows]
                later = [spread(lead[0][c], r) * inverse for c in range(r + 1, 8)]
                for k, q in enumerate(range(t, end)):
                    column = lead[k][r]
                    if k == 0:
                        column = jnp.where(sub > r, column, 0.0)
                    for c in range(r + 1, 8):
                        lead[k][c] = lead[k][c] - column * later[c - r - 1]
                    x[q] = [a - column * v for a, v in zip(x[q], rows)]
            band.append(jnp.concatenate(out, 1))
        band = jnp.concatenate(band, 0)
        done.append(band)
        if end < count:
            change = exact(band[:, :size], band, ((0,), (0,)))
            for q in range(end, count):
                x[q] = [x[q][n] - change[8 * q : 8 * q + 8, 128 * n : 128 * n + 128] for n in lanes]
    return jnp.concatenate(done, 0)


def factor_first_kernel(place, mine, theirs, first, rest, whole):
    core = place[1]
    h = mine.shape[0]
    whole[pl.ds(pl.multiple_of(core * h, h), h), :] = mine[...]
    whole[pl.ds(pl.multiple_of((1 - core) * h, h), h), :] = theirs[...]
    line = lax.broadcasted_iota(jnp.int32, (h, h), 0)
    lane = lax.broadcasted_iota(jnp.int32, (h, h), 1)
    eye = (line == lane).astype(F32)
    value = eliminate(jnp.concatenate([whole[:h, :], eye], 1), h)
    first[...] = value
    r12 = value[:, h : 2 * h]
    rest[...] = whole[h:, h:] - exact(r12, r12, ((0,), (0,)))


def factor_last_kernel(first, rest, triangle, inverse, turned):
    h = first.shape[0]
    line = lax.broadcasted_iota(jnp.int32, (h, h), 0)
    lane = lax.broadcasted_iota(jnp.int32, (h, h), 1)
    eye = (line == lane).astype(F32)
    zero = jnp.zeros((h, h), F32)
    second = eliminate(jnp.concatenate([rest[...], eye], 1), h)
    r11, r12, i11 = first[:, :h], first[:, h : 2 * h], first[:, 2 * h :]
    r22, i22 = second[:, :h], second[:, h:]
    i11 = jnp.where(lane <= line, i11, 0.0)
    i22 = jnp.where(lane <= line, i22, 0.0)
    i21 = -exact(i22, exact(r12, i11, ((0,), (0,))), ((1,), (0,)))
    triangle[:h, :h] = jnp.where(lane >= line, r11, 0.0)
    triangle[:h, h:] = r12
    triangle[h:, :h] = zero
    triangle[h:, h:] = jnp.where(lane >= line, r22, 0.0)
    full = jnp.concatenate([jnp.concatenate([i11, zero], 1), jnp.concatenate([i21, i22], 1)], 0)
    inverse[0], inverse[1] = split(full)
    turned[0], turned[1] = split(full.T)


def factor_first(place, mine, theirs):
    h, size = mine.shape
    return call(
        factor_first_kernel, (shape((h, 3 * h), F32), shape((h, h), F32)), [SMEM, VMEM, VMEM],
        (VMEM,) * 2, 8, flops=10 * size**3, moved=20 * MIB, scratch=(pltpu.VMEM((size, size), F32),),
    )(place, mine, theirs)


def factor_last(first, rest):
    size = 2 * first.shape[0]
    both = shape((2, size, size), BF16)
    return call(
        factor_last_kernel, (shape((size, size), F32), both, both), [VMEM, VMEM], (VMEM,) * 3, 8,
        flops=10 * size**3, moved=20 * MIB,
    )(first, rest)


def update_kernel(
    chips, place, inverse, turned, panel, near_one, far_one, near_two, far_two, active,
    top_out, out, sums, tops, results, top_sems, out_sems,
):
    core, chip = place[1], place[2]
    pair = lax.div(place[0], 2)
    rows, wide = results.shape[1:]
    steps = 2 * chips
    two = near_one.shape[1]
    rest = near_two.shape[1] // two
    block = rows // 4
    straight = ((1,), (0,))

    def where(i):
        side = core if i < chips else 1 - core
        return pl.ds(pl.multiple_of((side * chips + (chip ^ (i % chips))) * wide, wide), wide)

    def top_copy(i):
        return pltpu.make_async_copy(tops.at[i % 2], top_out.at[where(i), :], top_sems.at[i % 2])

    def out_copy(i):
        return pltpu.make_async_copy(results.at[i % 2], out.at[:, where(i)], out_sems.at[i % 2])

    def prepare(i):
        one, several = (near_one, near_two) if i < chips else (far_one, far_two)
        s = i % chips
        sums[i % 2, pl.ds(pl.multiple_of(pair * two, two), two), :] = one[s]
        for k in range(rest):
            q = k + (k >= pair).astype(jnp.int32)
            sums[i % 2, pl.ds(pl.multiple_of(q * two, two), two), :] = several[s, k * two : (k + 1) * two, :]
        cross = sums[i % 2]
        top = dot(inverse[0], cross, straight) + dot(inverse[1], cross, straight)
        high, low = split(top)
        tops[i % 2] = top.T
        return (
            dot(turned[0], high, straight) + (dot(turned[0], low, straight) + dot(turned[1], high, straight))
        ).astype(BF16)

    coeff = prepare(0)
    top_copy(0).start()
    for i in range(steps):
        if i >= 2:
            out_copy(i - 2).wait()
        if 1 <= i < steps - 1:
            top_copy(i - 1).wait()
        now = coeff
        if i + 1 < steps:
            coeff = prepare(i + 1)
        for k in range(0, rows, block):
            product = dot(panel[k : k + block, :], now, straight)
            results[i % 2, k : k + block, :] = (active[k : k + block, where(i)].astype(F32) - product).astype(BF16)
        if i + 1 < steps:
            top_copy(i + 1).start()
        out_copy(i).start()
    for i in (steps - 2, steps - 1):
        top_copy(i).wait()
        out_copy(i).wait()


def update(place, inverse, turned, panel, one, two, active, chips):
    rows, size = panel.shape
    columns = active.shape[1]
    wide = columns // (2 * chips)
    return call(
        functools.partial(update_kernel, chips),
        (shape((columns, size), F32), shape((rows, columns), BF16)),
        [SMEM] + [VMEM] * 8, (ANY, ANY), 12,
        flops=2 * rows * size * columns, moved=2 * rows * columns,
        scratch=(
            pltpu.VMEM((2, size, wide), BF16),
            pltpu.VMEM((2, wide, size), F32),
            pltpu.VMEM((2, rows, wide), BF16),
            pltpu.SemaphoreType.DMA((2,)),
            pltpu.SemaphoreType.DMA((2,)),
        ),
    )(place, inverse, turned, panel, *one, *two, active)


def local(nrow, ncol, panel, trailing, tile_list):
    row = lax.axis_index("row")
    place = jnp.stack([lax.axis_index("col"), row % 2, row // 2]).astype(jnp.int32)
    own = pick(tile_list, panel.T)
    blocks = [own]
    for s in range(1, ncol):
        blocks.append(lax.ppermute(own, "col", [(i, i ^ s) for i in range(ncol)]))
    across = 2 * panel.shape[1]
    active = load(tile_list, trailing)

    def both(prepare, deep, sources):
        send = swap(cross(prepare, False, deep, place, sources, active), 1, nrow)
        keep = cross(prepare, True, deep, place, sources, active)
        return reduce_cross(place, keep, send, nrow)

    one = both(pair_lhs, across, blocks[:2])
    full, keep, send = gram(place, blocks)
    sums = reduce_gram(keep, send, nrow)
    turned_panel = turn(full)
    two = both(rest_lhs, (ncol - 2) * panel.shape[1], [full])
    triangle, inverse, turned = factor_last(*factor_first(place, *sums))
    top_rows, updated = update(place, inverse, turned, turned_panel, one, two, active, nrow // 2)
    return triangle, top_rows, updated


def solution(mesh):
    nrow, ncol = mesh.shape["row"], mesh.shape["col"]

    def program(panel, trailing, tile_list):
        return local(nrow, ncol, panel, trailing, tile_list)

    return jax.shard_map(
        program,
        mesh=mesh,
        in_specs=(P("row", "col"), P("row", "col"), P("row")),
        out_specs=(P(), P("col", None), P("row", "col")),
        check_vma=False,
    )
```

```python
import functools
import jax
import jax.numpy as jnp
from jax import lax
from jax.sharding import PartitionSpec as P
from jax.experimental import pallas as pl
from jax.experimental.pallas import tpu as pltpu

TILE = 128
BAND = 4
F32 = jnp.float32
BF16 = jnp.bfloat16
VMEM = pl.BlockSpec(memory_space=pltpu.VMEM)
SMEM = pl.BlockSpec(memory_space=pltpu.SMEM)
ANY = pl.BlockSpec(memory_space=pl.ANY)
HBM = pl.BlockSpec(memory_space=pltpu.HBM)
MIB = 1 << 20


def shape(dims, kind):
    return jax.ShapeDtypeStruct(dims, kind)


def call(body, out_shape, in_specs, out_specs, grant, flops=0, moved=0, scratch=(), aliases=None):
    return pl.pallas_call(
        body,
        out_shape=out_shape,
        in_specs=in_specs,
        out_specs=out_specs,
        scratch_shapes=list(scratch),
        input_output_aliases=aliases or {},
        cost_estimate=pl.CostEstimate(flops=flops, bytes_accessed=moved, transcendentals=0),
        compiler_params=pltpu.CompilerParams(vmem_limit_bytes=grant * MIB),
    )


def stay(value):
    return pltpu.with_memory_space_constraint(value, pltpu.HBM)


def dot(a, b, contract):
    return lax.dot_general(a, b, (contract, ((), ())), preferred_element_type=F32)


def exact(a, b, contract):
    return lax.dot_general(
        a, b, (contract, ((), ())), precision=lax.Precision.HIGHEST, preferred_element_type=F32
    )


def split(value):
    high = value.astype(BF16)
    return high, (value - high.astype(F32)).astype(BF16)


def pick_kernel(listed, source, out, tiles, panel, sems):
    copies = (
        pltpu.make_async_copy(listed, tiles, sems.at[0]),
        pltpu.make_async_copy(source, panel, sems.at[1]),
    )
    for copy in copies:
        copy.start()
    for copy in copies:
        copy.wait()
    for k in range(tiles.shape[0]):
        start = pl.multiple_of(tiles[k] * TILE, TILE)
        out[:, k * TILE : (k + 1) * TILE] = panel[:, pl.ds(start, TILE)]


def pick(tile_list, panel):
    rows = tile_list.shape[0] * TILE
    return call(
        pick_kernel, shape((panel.shape[0], rows), BF16), [HBM, HBM], VMEM, 8,
        moved=4 * rows * panel.shape[0],
        scratch=(
            pltpu.SMEM(tile_list.shape, jnp.int32),
            pltpu.VMEM(panel.shape, BF16),
            pltpu.SemaphoreType.DMA((2,)),
        ),
    )(stay(tile_list), stay(panel))


def load_kernel(listed, trailing, active, tiles, sems):
    copy = pltpu.make_async_copy(listed, tiles, sems.at[0])
    copy.start()
    copy.wait()
    for k in range(tiles.shape[0]):
        start = pl.multiple_of(tiles[k] * TILE, TILE)
        pltpu.make_async_copy(
            trailing.at[pl.ds(start, TILE), :], active.at[pl.ds(k * TILE, TILE), :], sems.at[1]
        ).start()
    pltpu.make_async_copy(trailing.at[pl.ds(0, active.shape[0]), :], active, sems.at[1]).wait()


def load(tile_list, trailing):
    rows = tile_list.shape[0] * TILE
    columns = trailing.shape[1]
    return call(
        load_kernel, pltpu.VMEM((rows, columns), BF16), [HBM, HBM], VMEM, 8,
        moved=2 * rows * columns,
        scratch=(pltpu.SMEM(tile_list.shape, jnp.int32), pltpu.SemaphoreType.DMA((2,))),
    )(stay(tile_list), trailing)


def gram_kernel(relayed, place, *refs):
    *blocks, full, keep, send = refs
    z, core = place[0], place[1]
    wide = blocks[0].shape[0]
    if relayed:
        *blocks, inner, outer = blocks
        where = pl.ds(pl.multiple_of((z ^ len(blocks)) * wide, wide), wide)
        middle = jnp.logical_or(z == 1, z == 2)

        @pl.when(middle)
        def _():
            full[where, :] = inner[...]

        @pl.when(jnp.logical_not(middle))
        def _():
            full[where, :] = outer[...]

    for s, block in enumerate(blocks):
        full[pl.ds(pl.multiple_of((z ^ s) * wide, wide), wide), :] = block[...]
    half = keep.shape[0]
    everything = full[...]
    mine = full[pl.ds(pl.multiple_of(core * half, half), half), :]
    theirs = full[pl.ds(pl.multiple_of((1 - core) * half, half), half), :]
    send[...] = dot(theirs, everything, ((1,), (1,)))
    keep[...] = dot(mine, everything, ((1,), (1,)))


def gram(place, blocks, parts):
    wide, rows = blocks[0].shape
    width = parts * wide
    half = shape((width // 2, width), F32)
    return call(
        functools.partial(gram_kernel, len(blocks) > parts), (shape((width, rows), BF16), half, half),
        [SMEM] + [VMEM] * len(blocks), (VMEM, VMEM, VMEM), 16,
        flops=2 * width * width * rows, moved=4 * width * rows,
    )(place, *blocks)


def turn_kernel(full, out):
    step = 2 * TILE
    for k in range(full.shape[1] // step):
        out[k * step : (k + 1) * step, :] = full[:, k * step : (k + 1) * step].astype(F32).T.astype(BF16)


def turn(full):
    width, rows = full.shape
    return call(turn_kernel, shape((rows, width), BF16), [VMEM], VMEM, 16, moved=4 * width * rows)(full)


def pair_lhs(place, sources, lhs):
    odd = lax.rem(place[0], 2)
    for k, source in enumerate(sources):
        deep = source.shape[0]
        lhs[pl.ds(pl.multiple_of((odd ^ k) * deep, deep), deep), :] = source[...]


def rest_lhs(place, sources, lhs):
    (full,) = sources
    pair = lax.div(place[0], 2)
    across = full.shape[0] - lhs.shape[0]
    for k in range(lhs.shape[0] // across):
        q = k + (k >= pair).astype(jnp.int32)
        lhs[k * across : (k + 1) * across, :] = full[pl.ds(pl.multiple_of(q * across, across), across), :]


def cross_kernel(prepare, steps, mine, place, *refs):
    *sources, active, out, lhs = refs
    side = place[1] if mine else 1 - place[1]
    wide = out.shape[1] // steps
    prepare(place, sources, lhs)

    def body(i, _):
        source = pl.ds(pl.multiple_of(side * out.shape[1] + i * wide, wide), wide)
        where = pl.ds(pl.multiple_of(i * wide, wide), wide)
        out[:, where] = dot(lhs[...], active[:, source], ((1,), (0,))).astype(out.dtype)
        return 0

    lax.fori_loop(0, steps, body, 0)


def cross(prepare, mine, deep, place, sources, active):
    rows, columns = active.shape
    return call(
        functools.partial(cross_kernel, prepare, 4, mine),
        shape((deep, columns // 2), F32 if mine else BF16), [SMEM] + [VMEM] * (len(sources) + 1), VMEM, 8,
        flops=deep * rows * columns, moved=rows * columns,
        scratch=(pltpu.VMEM((deep, rows), BF16),),
    )(place, *sources, active)


def share_kernel(place, keep, got, own, *outs):
    chip = place[2]
    wide = own.shape[1]

    def total(where):
        return keep[:, where] + got[:, where].astype(F32)

    own[...] = total(pl.ds(pl.multiple_of(chip * wide, wide), wide))
    for s, out in enumerate(outs, 1):
        out[...] = total(pl.ds(pl.multiple_of((chip ^ s) * wide, wide), wide)).astype(BF16)


def share(place, keep, got, chips):
    deep, columns = keep.shape
    wide = columns // chips
    return call(
        share_kernel, [shape((deep, wide), F32)] + [shape((deep, wide), BF16)] * (chips - 1),
        [SMEM, VMEM, VMEM], [VMEM] * chips, 8, moved=8 * deep * columns,
    )(place, keep, got)


def swap(value, bit, rows):
    return lax.ppermute(value, "row", [(i, i ^ bit) for i in range(rows)])


def tree(values):
    values = [v.astype(F32) for v in values]
    while len(values) > 1:
        values = [a + b for a, b in zip(values[::2], values[1::2])]
    return values[0]


def bits_of(rows):
    return [1 << k for k in range(1, rows.bit_length() - 1)]


def reduce_cross(place, keep, got, rows):
    chips = rows // 2
    own, *outs = share(place, keep, got, chips)
    parts = [own] + [swap(v, 2 * s, rows) for s, v in enumerate(outs, 1)]
    return tree(parts).astype(BF16)


def gather_slow(mine, rows):
    stack = mine[None]
    for bit in bits_of(rows):
        other = swap(stack, bit, rows)
        stack = jnp.concatenate([stack, other], 0)
    return stack


def gather_fast(mine, rows):
    return [mine] + [swap(mine, 2 * s, rows) for s in range(1, rows // 2)]


def reduce_gram(keep, send, rows):
    own = keep + swap(send, 1, rows)
    parts = [own] + [swap(own, 2 * s, rows) for s in range(1, rows // 2)]
    total = tree(parts)
    return total, swap(total, 1, rows)


def spread(value, r):
    return jnp.broadcast_to(value[r : r + 1, :], (8, 128))


def eliminate(value, size):
    sub = lax.broadcasted_iota(jnp.int32, (8, 128), 0)
    lanes = range(value.shape[1] // 128)
    count = size // 8
    span = min(BAND, count)
    x = [[value[8 * q : 8 * q + 8, 128 * n : 128 * n + 128] for n in lanes] for q in range(count)]
    done = []
    for begin in range(0, count, span):
        end = begin + span
        band = []
        for t in range(begin, end):
            group, at = divmod(8 * t, 128)
            lead = [
                [jnp.broadcast_to(x[q][group][:, at + c : at + c + 1], (8, 128)) for c in range(8)]
                for q in range(t, end)
            ]
            out = [jnp.zeros((8, 128), F32) for _ in lanes]
            for r in range(8):
                root = lax.rsqrt(spread(lead[0][r], r))
                inverse = root * root
                rows = [spread(x[t][n], r) for n in lanes]
                out = [jnp.where(sub == r, v * root, o) for v, o in zip(rows, out)]
                rows = [v * inverse for v in rows]
                later = [spread(lead[0][c], r) * inverse for c in range(r + 1, 8)]
                for k, q in enumerate(range(t, end)):
                    column = lead[k][r]
                    if k == 0:
                        column = jnp.where(sub > r, column, 0.0)
                    for c in range(r + 1, 8):
                        lead[k][c] = lead[k][c] - column * later[c - r - 1]
                    x[q] = [a - column * v for a, v in zip(x[q], rows)]
            band.append(jnp.concatenate(out, 1))
        band = jnp.concatenate(band, 0)
        done.append(band)
        if end < count:
            change = exact(band[:, :size], band, ((0,), (0,)))
            for q in range(end, count):
                x[q] = [x[q][n] - change[8 * q : 8 * q + 8, 128 * n : 128 * n + 128] for n in lanes]
    return jnp.concatenate(done, 0)


def factor_first_kernel(place, mine, theirs, first, rest, whole):
    core = place[1]
    h = mine.shape[0]
    whole[pl.ds(pl.multiple_of(core * h, h), h), :] = mine[...]
    whole[pl.ds(pl.multiple_of((1 - core) * h, h), h), :] = theirs[...]
    line = lax.broadcasted_iota(jnp.int32, (h, h), 0)
    lane = lax.broadcasted_iota(jnp.int32, (h, h), 1)
    eye = (line == lane).astype(F32)
    value = eliminate(jnp.concatenate([whole[:h, :], eye], 1), h)
    first[...] = value
    r12 = value[:, h : 2 * h]
    rest[...] = whole[h:, h:] - exact(r12, r12, ((0,), (0,)))


def factor_last_kernel(first, rest, triangle, inverse, turned):
    h = first.shape[0]
    line = lax.broadcasted_iota(jnp.int32, (h, h), 0)
    lane = lax.broadcasted_iota(jnp.int32, (h, h), 1)
    eye = (line == lane).astype(F32)
    zero = jnp.zeros((h, h), F32)
    second = eliminate(jnp.concatenate([rest[...], eye], 1), h)
    r11, r12, i11 = first[:, :h], first[:, h : 2 * h], first[:, 2 * h :]
    r22, i22 = second[:, :h], second[:, h:]
    i11 = jnp.where(lane <= line, i11, 0.0)
    i22 = jnp.where(lane <= line, i22, 0.0)
    i21 = -exact(i22, exact(r12, i11, ((0,), (0,))), ((1,), (0,)))
    triangle[:h, :h] = jnp.where(lane >= line, r11, 0.0)
    triangle[:h, h:] = r12
    triangle[h:, :h] = zero
    triangle[h:, h:] = jnp.where(lane >= line, r22, 0.0)
    full = jnp.concatenate([jnp.concatenate([i11, zero], 1), jnp.concatenate([i21, i22], 1)], 0)
    inverse[0], inverse[1] = split(full)
    turned[0], turned[1] = split(full.T)


def factor_first(place, mine, theirs):
    h, size = mine.shape
    return call(
        factor_first_kernel, (shape((h, 3 * h), F32), shape((h, h), F32)), [SMEM, VMEM, VMEM],
        (VMEM,) * 2, 8, flops=10 * size**3, moved=20 * MIB, scratch=(pltpu.VMEM((size, size), F32),),
    )(place, mine, theirs)


def factor_last(first, rest):
    size = 2 * first.shape[0]
    both = shape((2, size, size), BF16)
    return call(
        factor_last_kernel, (shape((size, size), F32), both, both), [VMEM, VMEM], (VMEM,) * 3, 8,
        flops=10 * size**3, moved=20 * MIB,
    )(first, rest)


def coeff_kernel(place, inverse, turned, one, *refs):
    *several, top_out, coeff_out, sums = refs
    pair = lax.div(place[0], 2)
    two, wide = one.shape[1:]
    straight = ((1,), (0,))
    for s, other in enumerate(several):
        sums[s % 2, pl.ds(pl.multiple_of(pair * two, two), two), :] = one[s]
        for k in range(other.shape[0] // two):
            q = k + (k >= pair).astype(jnp.int32)
            sums[s % 2, pl.ds(pl.multiple_of(q * two, two), two), :] = other[k * two : (k + 1) * two, :]
        cross = sums[s % 2]
        top = dot(inverse[0], cross, straight) + dot(inverse[1], cross, straight)
        high, low = split(top)
        part = slice(s * wide, (s + 1) * wide)
        top_out[part, :] = top.T
        coeff_out[:, part] = (
            dot(turned[0], high, straight) + (dot(turned[0], low, straight) + dot(turned[1], high, straight))
        ).astype(BF16)


def coefficients(place, inverse, turned, one, several):
    size = inverse.shape[1]
    wide = one.shape[2]
    half = wide * len(several)
    return call(
        coeff_kernel, (shape((half, size), F32), shape((size, half), BF16)),
        [SMEM] + [VMEM] * (3 + len(several)), (VMEM, VMEM), 12,
        flops=10 * size * size * half, moved=8 * size * half, scratch=(pltpu.VMEM((2, size, wide), BF16),),
    )(place, inverse, turned, one, *several)


def update_kernel(chips, mine, place, panel, coeff, top, active, *refs):
    top_out, out, results, top_sem, out_sems = refs[-5:]
    chip = place[2]
    side = place[1] if mine else 1 - place[1]
    rows, wide = results.shape[1:]
    block = rows // 4

    def where(s):
        return pl.ds(pl.multiple_of((side * chips + (chip ^ s)) * wide, wide), wide)

    def top_copy(s):
        return pltpu.make_async_copy(top.at[pl.ds(s * wide, wide), :], top_out.at[where(s), :], top_sem)

    def out_copy(s, part):
        return pltpu.make_async_copy(results.at[s % 2, part, :], out.at[part, where(s)], out_sems.at[s % 2])

    for s in range(chips):
        top_copy(s).start()
    for s in range(chips):
        if s >= 2:
            out_copy(s - 2, pl.ds(0, rows)).wait()
        weights = coeff[:, s * wide : (s + 1) * wide]
        for k in range(0, rows, block):
            product = dot(panel[k : k + block, :], weights, ((1,), (0,)))
            results[s % 2, k : k + block, :] = (active[k : k + block, where(s)].astype(F32) - product).astype(BF16)
            out_copy(s, pl.ds(k, block)).start()
    for s in range(max(chips - 2, 0), chips):
        out_copy(s, pl.ds(0, rows)).wait()
    half = chips * wide
    pltpu.make_async_copy(top, top_out.at[pl.ds(0, half), :], top_sem).wait()


def update(mine, chips, place, panel, coeff, top, active, before=()):
    rows, size = panel.shape
    columns = active.shape[1]
    wide = columns // (2 * chips)
    return call(
        functools.partial(update_kernel, chips, mine),
        (shape((columns, size), F32), shape((rows, columns), BF16)),
        [SMEM] + [VMEM] * 4 + [ANY] * len(before), (ANY, ANY), 12,
        flops=rows * size * columns, moved=rows * columns,
        scratch=(
            pltpu.VMEM((2, rows, wide), BF16),
            pltpu.SemaphoreType.DMA(()),
            pltpu.SemaphoreType.DMA((2,)),
        ),
        aliases={5: 0, 6: 1} if before else None,
    )(place, panel, coeff, top, active, *before)


def gather_panel(own, ncol):
    def shift(value, pairs):
        return lax.ppermute(value, "col", pairs)

    def direct(s):
        return shift(own, [(i, i ^ s) for i in range(ncol)])

    if ncol != 4:
        return [own] + [direct(s) for s in range(1, ncol)]
    across = direct(2)
    return [own, direct(1), across, shift(own, [(1, 2), (2, 1)]), shift(across, [(2, 3), (1, 0)])]


def local(nrow, ncol, panel, trailing, tile_list):
    row = lax.axis_index("row")
    place = jnp.stack([lax.axis_index("col"), row % 2, row // 2]).astype(jnp.int32)
    chips = nrow // 2
    own = pick(tile_list, panel.T)
    blocks = gather_panel(own, ncol)
    across = 2 * panel.shape[1]
    active = load(tile_list, trailing)

    def both(prepare, deep, sources):
        send = swap(cross(prepare, False, deep, place, sources, active), 1, nrow)
        keep = cross(prepare, True, deep, place, sources, active)
        return reduce_cross(place, keep, send, nrow)

    one = gather_slow(both(pair_lhs, across, blocks[:2]), nrow)
    full, keep, send = gram(place, blocks, ncol)
    sums = reduce_gram(keep, send, nrow)
    turned_panel = turn(full)
    two = gather_fast(both(rest_lhs, (ncol - 2) * panel.shape[1], [full]), nrow)
    triangle, inverse, turned = factor_last(*factor_first(place, *sums))
    top, coeff = coefficients(place, inverse, turned, one, two)
    outs = update(True, chips, place, turned_panel, coeff, top, active)
    coeff, top = swap(coeff, 1, nrow), swap(top, 1, nrow)
    top_rows, updated = update(False, chips, place, turned_panel, coeff, top, active, outs)
    return triangle, top_rows, updated


def solution(mesh):
    nrow, ncol = mesh.shape["row"], mesh.shape["col"]

    def program(panel, trailing, tile_list):
        return local(nrow, ncol, panel, trailing, tile_list)

    return jax.shard_map(
        program,
        mesh=mesh,
        in_specs=(P("row", "col"), P("row", "col"), P("row")),
        out_specs=(P(), P("col", None), P("row", "col")),
        check_vma=False,
    )
```

```python
import functools
import jax
import jax.numpy as jnp
from jax import lax
from jax.sharding import PartitionSpec as P
from jax.experimental import pallas as pl
from jax.experimental.pallas import tpu as pltpu

TILE = 128
BAND = 4
F32 = jnp.float32
BF16 = jnp.bfloat16
VMEM = pl.BlockSpec(memory_space=pltpu.VMEM)
SMEM = pl.BlockSpec(memory_space=pltpu.SMEM)
ANY = pl.BlockSpec(memory_space=pl.ANY)
HBM = pl.BlockSpec(memory_space=pltpu.HBM)
MIB = 1 << 20


def shape(dims, kind):
    return jax.ShapeDtypeStruct(dims, kind)


def call(body, out_shape, in_specs, out_specs, grant, flops=0, moved=0, scratch=(), aliases=None):
    return pl.pallas_call(
        body,
        out_shape=out_shape,
        in_specs=in_specs,
        out_specs=out_specs,
        scratch_shapes=list(scratch),
        input_output_aliases=aliases or {},
        cost_estimate=pl.CostEstimate(flops=flops, bytes_accessed=moved, transcendentals=0),
        compiler_params=pltpu.CompilerParams(vmem_limit_bytes=grant * MIB),
    )


def stay(value):
    return pltpu.with_memory_space_constraint(value, pltpu.HBM)


def dot(a, b, contract):
    return lax.dot_general(a, b, (contract, ((), ())), preferred_element_type=F32)


def exact(a, b, contract):
    return lax.dot_general(
        a, b, (contract, ((), ())), precision=lax.Precision.HIGHEST, preferred_element_type=F32
    )


def split(value):
    high = value.astype(BF16)
    return high, (value - high.astype(F32)).astype(BF16)


def pick_kernel(listed, source, out, tiles, panel, sems):
    copies = (
        pltpu.make_async_copy(listed, tiles, sems.at[0]),
        pltpu.make_async_copy(source, panel, sems.at[1]),
    )
    for copy in copies:
        copy.start()
    for copy in copies:
        copy.wait()
    for k in range(tiles.shape[0]):
        start = pl.multiple_of(tiles[k] * TILE, TILE)
        out[:, k * TILE : (k + 1) * TILE] = panel[:, pl.ds(start, TILE)]


def pick(tile_list, panel):
    rows = tile_list.shape[0] * TILE
    return call(
        pick_kernel, shape((panel.shape[0], rows), BF16), [HBM, HBM], VMEM, 8,
        moved=4 * rows * panel.shape[0],
        scratch=(
            pltpu.SMEM(tile_list.shape, jnp.int32),
            pltpu.VMEM(panel.shape, BF16),
            pltpu.SemaphoreType.DMA((2,)),
        ),
    )(stay(tile_list), stay(panel))


def load_kernel(listed, trailing, active, tiles, sems):
    copy = pltpu.make_async_copy(listed, tiles, sems.at[0])
    copy.start()
    copy.wait()
    for k in range(tiles.shape[0]):
        start = pl.multiple_of(tiles[k] * TILE, TILE)
        pltpu.make_async_copy(
            trailing.at[pl.ds(start, TILE), :], active.at[pl.ds(k * TILE, TILE), :], sems.at[1]
        ).start()
    pltpu.make_async_copy(trailing.at[pl.ds(0, active.shape[0]), :], active, sems.at[1]).wait()


def load(tile_list, trailing):
    rows = tile_list.shape[0] * TILE
    columns = trailing.shape[1]
    return call(
        load_kernel, pltpu.VMEM((rows, columns), BF16), [HBM, HBM], VMEM, 8,
        moved=2 * rows * columns,
        scratch=(pltpu.SMEM(tile_list.shape, jnp.int32), pltpu.SemaphoreType.DMA((2,))),
    )(stay(tile_list), trailing)


def gram_kernel(relayed, place, *refs):
    *blocks, full, keep, send = refs
    z, core = place[0], place[1]
    wide = blocks[0].shape[0]
    if relayed:
        *blocks, inner, outer = blocks
        where = pl.ds(pl.multiple_of((z ^ len(blocks)) * wide, wide), wide)
        middle = jnp.logical_or(z == 1, z == 2)

        @pl.when(middle)
        def _():
            full[where, :] = inner[...]

        @pl.when(jnp.logical_not(middle))
        def _():
            full[where, :] = outer[...]

    for s, block in enumerate(blocks):
        full[pl.ds(pl.multiple_of((z ^ s) * wide, wide), wide), :] = block[...]
    half = keep.shape[0]
    everything = full[...]
    mine = full[pl.ds(pl.multiple_of(core * half, half), half), :]
    theirs = full[pl.ds(pl.multiple_of((1 - core) * half, half), half), :]
    send[...] = dot(theirs, everything, ((1,), (1,)))
    keep[...] = dot(mine, everything, ((1,), (1,)))


def gram(place, blocks, parts):
    wide, rows = blocks[0].shape
    width = parts * wide
    half = shape((width // 2, width), F32)
    return call(
        functools.partial(gram_kernel, len(blocks) > parts), (shape((width, rows), BF16), half, half),
        [SMEM] + [VMEM] * len(blocks), (VMEM, VMEM, VMEM), 16,
        flops=2 * width * width * rows, moved=4 * width * rows,
    )(place, *blocks)


def turn_kernel(full, out):
    step = 2 * TILE
    for k in range(full.shape[1] // step):
        out[k * step : (k + 1) * step, :] = full[:, k * step : (k + 1) * step].astype(F32).T.astype(BF16)


def turn(full):
    width, rows = full.shape
    return call(turn_kernel, shape((rows, width), BF16), [VMEM], VMEM, 16, moved=4 * width * rows)(full)


def pair_lhs(place, sources, lhs):
    odd = lax.rem(place[0], 2)
    for k, source in enumerate(sources):
        deep = source.shape[0]
        lhs[pl.ds(pl.multiple_of((odd ^ k) * deep, deep), deep), :] = source[...]


def rest_lhs(place, sources, lhs):
    (full,) = sources
    pair = lax.div(place[0], 2)
    across = full.shape[0] - lhs.shape[0]
    for k in range(lhs.shape[0] // across):
        q = k + (k >= pair).astype(jnp.int32)
        lhs[k * across : (k + 1) * across, :] = full[pl.ds(pl.multiple_of(q * across, across), across), :]


def cross_kernel(prepare, steps, mine, place, *refs):
    *sources, active, out, lhs = refs
    side = place[1] if mine else 1 - place[1]
    wide = out.shape[1] // steps
    prepare(place, sources, lhs)

    def body(i, _):
        source = pl.ds(pl.multiple_of(side * out.shape[1] + i * wide, wide), wide)
        where = pl.ds(pl.multiple_of(i * wide, wide), wide)
        out[:, where] = dot(lhs[...], active[:, source], ((1,), (0,))).astype(out.dtype)
        return 0

    lax.fori_loop(0, steps, body, 0)


def cross(prepare, mine, deep, place, sources, active):
    rows, columns = active.shape
    return call(
        functools.partial(cross_kernel, prepare, 4, mine),
        shape((deep, columns // 2), F32 if mine else BF16), [SMEM] + [VMEM] * (len(sources) + 1), VMEM, 8,
        flops=deep * rows * columns, moved=rows * columns,
        scratch=(pltpu.VMEM((deep, rows), BF16),),
    )(place, *sources, active)


def share_kernel(place, keep, got, own, *outs):
    chip = place[2]
    wide = own.shape[1]

    def total(where):
        return keep[:, where] + got[:, where].astype(F32)

    own[...] = total(pl.ds(pl.multiple_of(chip * wide, wide), wide))
    for s, out in enumerate(outs, 1):
        out[...] = total(pl.ds(pl.multiple_of((chip ^ s) * wide, wide), wide)).astype(BF16)


def share(place, keep, got, chips):
    deep, columns = keep.shape
    wide = columns // chips
    return call(
        share_kernel, [shape((deep, wide), F32)] + [shape((deep, wide), BF16)] * (chips - 1),
        [SMEM, VMEM, VMEM], [VMEM] * chips, 8, moved=8 * deep * columns,
    )(place, keep, got)


def swap(value, bit, rows):
    return lax.ppermute(value, "row", [(i, i ^ bit) for i in range(rows)])


def tree(values):
    values = [v.astype(F32) for v in values]
    while len(values) > 1:
        values = [a + b for a, b in zip(values[::2], values[1::2])]
    return values[0]


def bits_of(rows):
    return [1 << k for k in range(1, rows.bit_length() - 1)]


def reduce_cross(place, keep, got, rows):
    chips = rows // 2
    own, *outs = share(place, keep, got, chips)
    parts = [own] + [swap(v, 2 * s, rows) for s, v in enumerate(outs, 1)]
    return tree(parts).astype(BF16)


def gather_slow(mine, rows):
    stack = mine[None]
    for bit in bits_of(rows):
        other = swap(stack, bit, rows)
        stack = jnp.concatenate([stack, other], 0)
    return stack


def gather_fast(mine, rows):
    return [mine] + [swap(mine, 2 * s, rows) for s in range(1, rows // 2)]


def reduce_gram(keep, send, rows):
    own = keep + swap(send, 1, rows)
    parts = [own] + [swap(own, 2 * s, rows) for s in range(1, rows // 2)]
    total = tree(parts)
    return total, swap(total, 1, rows)


def spread(value, r):
    return jnp.broadcast_to(value[r : r + 1, :], (8, 128))


def eliminate(value, size):
    sub = lax.broadcasted_iota(jnp.int32, (8, 128), 0)
    lanes = range(value.shape[1] // 128)
    count = size // 8
    span = min(BAND, count)
    x = [[value[8 * q : 8 * q + 8, 128 * n : 128 * n + 128] for n in lanes] for q in range(count)]
    done = []
    for begin in range(0, count, span):
        end = begin + span
        band = []
        for t in range(begin, end):
            group, at = divmod(8 * t, 128)
            lead = [
                [jnp.broadcast_to(x[q][group][:, at + c : at + c + 1], (8, 128)) for c in range(8)]
                for q in range(t, end)
            ]
            out = [jnp.zeros((8, 128), F32) for _ in lanes]
            for r in range(8):
                root = lax.rsqrt(spread(lead[0][r], r))
                inverse = root * root
                rows = [spread(x[t][n], r) for n in lanes]
                out = [jnp.where(sub == r, v * root, o) for v, o in zip(rows, out)]
                rows = [v * inverse for v in rows]
                later = [spread(lead[0][c], r) * inverse for c in range(r + 1, 8)]
                for k, q in enumerate(range(t, end)):
                    column = lead[k][r]
                    if k == 0:
                        column = jnp.where(sub > r, column, 0.0)
                    for c in range(r + 1, 8):
                        lead[k][c] = lead[k][c] - column * later[c - r - 1]
                    x[q] = [a - column * v for a, v in zip(x[q], rows)]
            band.append(jnp.concatenate(out, 1))
        band = jnp.concatenate(band, 0)
        done.append(band)
        if end < count:
            change = exact(band[:, :size].T[8 * end :, :], band, ((1,), (0,)))
            for q in range(end, count):
                k = 8 * (q - end)
                x[q] = [x[q][n] - change[k : k + 8, 128 * n : 128 * n + 128] for n in lanes]
    return jnp.concatenate(done, 0)


def factor_first_kernel(place, mine, theirs, first, rest, whole):
    core = place[1]
    h = mine.shape[0]
    whole[pl.ds(pl.multiple_of(core * h, h), h), :] = mine[...]
    whole[pl.ds(pl.multiple_of((1 - core) * h, h), h), :] = theirs[...]
    line = lax.broadcasted_iota(jnp.int32, (h, h), 0)
    lane = lax.broadcasted_iota(jnp.int32, (h, h), 1)
    eye = (line == lane).astype(F32)
    value = eliminate(jnp.concatenate([whole[:h, :], eye], 1), h)
    first[...] = value
    r12 = value[:, h : 2 * h]
    rest[...] = whole[h:, h:] - exact(r12, r12, ((0,), (0,)))


def factor_last_kernel(first, rest, triangle, inverse, turned):
    h = first.shape[0]
    line = lax.broadcasted_iota(jnp.int32, (h, h), 0)
    lane = lax.broadcasted_iota(jnp.int32, (h, h), 1)
    eye = (line == lane).astype(F32)
    zero = jnp.zeros((h, h), F32)
    second = eliminate(jnp.concatenate([rest[...], eye], 1), h)
    r11, r12, i11 = first[:, :h], first[:, h : 2 * h], first[:, 2 * h :]
    r22, i22 = second[:, :h], second[:, h:]
    i11 = jnp.where(lane <= line, i11, 0.0)
    i22 = jnp.where(lane <= line, i22, 0.0)
    i21 = -exact(i22, exact(r12, i11, ((0,), (0,))), ((1,), (0,)))
    triangle[:h, :h] = jnp.where(lane >= line, r11, 0.0)
    triangle[:h, h:] = r12
    triangle[h:, :h] = zero
    triangle[h:, h:] = jnp.where(lane >= line, r22, 0.0)
    full = jnp.concatenate([jnp.concatenate([i11, zero], 1), jnp.concatenate([i21, i22], 1)], 0)
    inverse[0], inverse[1] = split(full)
    turned[0], turned[1] = split(full.T)


def factor_first(place, mine, theirs):
    h, size = mine.shape
    return call(
        factor_first_kernel, (shape((h, 3 * h), F32), shape((h, h), F32)), [SMEM, VMEM, VMEM],
        (VMEM,) * 2, 8, flops=10 * size**3, moved=20 * MIB, scratch=(pltpu.VMEM((size, size), F32),),
    )(place, mine, theirs)


def factor_last(first, rest):
    size = 2 * first.shape[0]
    both = shape((2, size, size), BF16)
    return call(
        factor_last_kernel, (shape((size, size), F32), both, both), [VMEM, VMEM], (VMEM,) * 3, 8,
        flops=10 * size**3, moved=20 * MIB,
    )(first, rest)


def coeff_kernel(place, inverse, turned, one, *refs):
    *several, top_out, coeff_out, sums = refs
    pair = lax.div(place[0], 2)
    two, wide = one.shape[1:]
    straight = ((1,), (0,))
    for s, other in enumerate(several):
        sums[s % 2, pl.ds(pl.multiple_of(pair * two, two), two), :] = one[s]
        for k in range(other.shape[0] // two):
            q = k + (k >= pair).astype(jnp.int32)
            sums[s % 2, pl.ds(pl.multiple_of(q * two, two), two), :] = other[k * two : (k + 1) * two, :]
        cross = sums[s % 2]
        top = dot(inverse[0], cross, straight) + dot(inverse[1], cross, straight)
        high, low = split(top)
        part = slice(s * wide, (s + 1) * wide)
        top_out[part, :] = top.T
        coeff_out[:, part] = (
            dot(turned[0], high, straight) + (dot(turned[0], low, straight) + dot(turned[1], high, straight))
        ).astype(BF16)


def coefficients(place, inverse, turned, one, several):
    size = inverse.shape[1]
    wide = one.shape[2]
    half = wide * len(several)
    return call(
        coeff_kernel, (shape((half, size), F32), shape((size, half), BF16)),
        [SMEM] + [VMEM] * (3 + len(several)), (VMEM, VMEM), 12,
        flops=10 * size * size * half, moved=8 * size * half, scratch=(pltpu.VMEM((2, size, wide), BF16),),
    )(place, inverse, turned, one, *several)


def update_kernel(chips, mine, place, panel, coeff, top, active, *refs):
    top_out, out, results, top_sem, out_sems = refs[-5:]
    chip = place[2]
    side = place[1] if mine else 1 - place[1]
    rows, wide = results.shape[1:]
    block = rows // 4

    def where(s):
        return pl.ds(pl.multiple_of((side * chips + (chip ^ s)) * wide, wide), wide)

    def top_copy(s):
        return pltpu.make_async_copy(top.at[pl.ds(s * wide, wide), :], top_out.at[where(s), :], top_sem)

    def out_copy(s, part):
        return pltpu.make_async_copy(results.at[s % 2, part, :], out.at[part, where(s)], out_sems.at[s % 2])

    for s in range(chips):
        top_copy(s).start()
    for s in range(chips):
        if s >= 2:
            out_copy(s - 2, pl.ds(0, rows)).wait()
        weights = coeff[:, s * wide : (s + 1) * wide]
        for k in range(0, rows, block):
            product = dot(panel[k : k + block, :], weights, ((1,), (0,)))
            results[s % 2, k : k + block, :] = (active[k : k + block, where(s)].astype(F32) - product).astype(BF16)
            out_copy(s, pl.ds(k, block)).start()
    for s in range(max(chips - 2, 0), chips):
        out_copy(s, pl.ds(0, rows)).wait()
    half = chips * wide
    pltpu.make_async_copy(top, top_out.at[pl.ds(0, half), :], top_sem).wait()


def update(mine, chips, place, panel, coeff, top, active, before=()):
    rows, size = panel.shape
    columns = active.shape[1]
    wide = columns // (2 * chips)
    return call(
        functools.partial(update_kernel, chips, mine),
        (shape((columns, size), F32), shape((rows, columns), BF16)),
        [SMEM] + [VMEM] * 4 + [ANY] * len(before), (ANY, ANY), 12,
        flops=rows * size * columns, moved=rows * columns,
        scratch=(
            pltpu.VMEM((2, rows, wide), BF16),
            pltpu.SemaphoreType.DMA(()),
            pltpu.SemaphoreType.DMA((2,)),
        ),
        aliases={5: 0, 6: 1} if before else None,
    )(place, panel, coeff, top, active, *before)


def gather_panel(own, ncol):
    def shift(value, pairs):
        return lax.ppermute(value, "col", pairs)

    def direct(s):
        return shift(own, [(i, i ^ s) for i in range(ncol)])

    if ncol != 4:
        return [own] + [direct(s) for s in range(1, ncol)]
    across = direct(2)
    return [own, direct(1), across, shift(own, [(1, 2), (2, 1)]), shift(across, [(2, 3), (1, 0)])]


def local(nrow, ncol, panel, trailing, tile_list):
    row = lax.axis_index("row")
    place = jnp.stack([lax.axis_index("col"), row % 2, row // 2]).astype(jnp.int32)
    chips = nrow // 2
    own = pick(tile_list, panel.T)
    blocks = gather_panel(own, ncol)
    across = 2 * panel.shape[1]
    active = load(tile_list, trailing)

    def both(prepare, deep, sources):
        send = swap(cross(prepare, False, deep, place, sources, active), 1, nrow)
        keep = cross(prepare, True, deep, place, sources, active)
        return reduce_cross(place, keep, send, nrow)

    one = gather_slow(both(pair_lhs, across, blocks[:2]), nrow)
    full, keep, send = gram(place, blocks, ncol)
    sums = reduce_gram(keep, send, nrow)
    turned_panel = turn(full)
    two = gather_fast(both(rest_lhs, (ncol - 2) * panel.shape[1], [full]), nrow)
    triangle, inverse, turned = factor_last(*factor_first(place, *sums))
    top, coeff = coefficients(place, inverse, turned, one, two)
    outs = update(True, chips, place, turned_panel, coeff, top, active)
    coeff, top = swap(coeff, 1, nrow), swap(top, 1, nrow)
    top_rows, updated = update(False, chips, place, turned_panel, coeff, top, active, outs)
    return triangle, top_rows, updated


def solution(mesh):
    nrow, ncol = mesh.shape["row"], mesh.shape["col"]

    def program(panel, trailing, tile_list):
        return local(nrow, ncol, panel, trailing, tile_list)

    return jax.shard_map(
        program,
        mesh=mesh,
        in_specs=(P("row", "col"), P("row", "col"), P("row")),
        out_specs=(P(), P("col", None), P("row", "col")),
        check_vma=False,
    )
```

```python
import functools
import jax
import jax.numpy as jnp
from jax import lax
from jax.sharding import PartitionSpec as P
from jax.experimental import pallas as pl
from jax.experimental.pallas import tpu as pltpu

TILE = 128
BAND = 4
F32 = jnp.float32
BF16 = jnp.bfloat16
VMEM = pl.BlockSpec(memory_space=pltpu.VMEM)
SMEM = pl.BlockSpec(memory_space=pltpu.SMEM)
ANY = pl.BlockSpec(memory_space=pl.ANY)
HBM = pl.BlockSpec(memory_space=pltpu.HBM)
MIB = 1 << 20


def shape(dims, kind):
    return jax.ShapeDtypeStruct(dims, kind)


def call(body, out_shape, in_specs, out_specs, grant, flops=0, moved=0, scratch=(), aliases=None):
    return pl.pallas_call(
        body,
        out_shape=out_shape,
        in_specs=in_specs,
        out_specs=out_specs,
        scratch_shapes=list(scratch),
        input_output_aliases=aliases or {},
        cost_estimate=pl.CostEstimate(flops=flops, bytes_accessed=moved, transcendentals=0),
        compiler_params=pltpu.CompilerParams(vmem_limit_bytes=grant * MIB),
    )


def stay(value):
    return pltpu.with_memory_space_constraint(value, pltpu.HBM)


def dot(a, b, contract):
    return lax.dot_general(a, b, (contract, ((), ())), preferred_element_type=F32)


def exact(a, b, contract):
    return lax.dot_general(
        a, b, (contract, ((), ())), precision=lax.Precision.HIGHEST, preferred_element_type=F32
    )


def split(value):
    high = value.astype(BF16)
    return high, (value - high.astype(F32)).astype(BF16)


def pick_kernel(listed, source, out, tiles, panel, sems):
    copies = (
        pltpu.make_async_copy(listed, tiles, sems.at[0]),
        pltpu.make_async_copy(source, panel, sems.at[1]),
    )
    for copy in copies:
        copy.start()
    for copy in copies:
        copy.wait()
    for k in range(tiles.shape[0]):
        start = pl.multiple_of(tiles[k] * TILE, TILE)
        out[:, k * TILE : (k + 1) * TILE] = panel[:, pl.ds(start, TILE)]


def pick(tile_list, panel):
    rows = tile_list.shape[0] * TILE
    return call(
        pick_kernel, shape((panel.shape[0], rows), BF16), [HBM, HBM], VMEM, 8,
        moved=4 * rows * panel.shape[0],
        scratch=(
            pltpu.SMEM(tile_list.shape, jnp.int32),
            pltpu.VMEM(panel.shape, BF16),
            pltpu.SemaphoreType.DMA((2,)),
        ),
    )(stay(tile_list), stay(panel))


def load_kernel(listed, trailing, active, tiles, sems):
    copy = pltpu.make_async_copy(listed, tiles, sems.at[0])
    copy.start()
    copy.wait()
    for k in range(tiles.shape[0]):
        start = pl.multiple_of(tiles[k] * TILE, TILE)
        pltpu.make_async_copy(
            trailing.at[pl.ds(start, TILE), :], active.at[pl.ds(k * TILE, TILE), :], sems.at[1]
        ).start()
    pltpu.make_async_copy(trailing.at[pl.ds(0, active.shape[0]), :], active, sems.at[1]).wait()


def load(tile_list, trailing):
    rows = tile_list.shape[0] * TILE
    columns = trailing.shape[1]
    return call(
        load_kernel, pltpu.VMEM((rows, columns), BF16), [HBM, HBM], VMEM, 8,
        moved=2 * rows * columns,
        scratch=(pltpu.SMEM(tile_list.shape, jnp.int32), pltpu.SemaphoreType.DMA((2,))),
    )(stay(tile_list), trailing)


def gram_kernel(relayed, place, *refs):
    *blocks, full, keep, send = refs
    z, core = place[0], place[1]
    wide = blocks[0].shape[0]
    if relayed:
        *blocks, inner, outer = blocks
        where = pl.ds(pl.multiple_of((z ^ len(blocks)) * wide, wide), wide)
        middle = jnp.logical_or(z == 1, z == 2)

        @pl.when(middle)
        def _():
            full[where, :] = inner[...]

        @pl.when(jnp.logical_not(middle))
        def _():
            full[where, :] = outer[...]

    for s, block in enumerate(blocks):
        full[pl.ds(pl.multiple_of((z ^ s) * wide, wide), wide), :] = block[...]
    half = keep.shape[0]
    everything = full[...]
    mine = full[pl.ds(pl.multiple_of(core * half, half), half), :]
    theirs = full[pl.ds(pl.multiple_of((1 - core) * half, half), half), :]
    send[...] = dot(theirs, everything, ((1,), (1,)))
    keep[...] = dot(mine, everything, ((1,), (1,)))


def gram(place, blocks, parts):
    wide, rows = blocks[0].shape
    width = parts * wide
    half = shape((width // 2, width), F32)
    return call(
        functools.partial(gram_kernel, len(blocks) > parts), (shape((width, rows), BF16), half, half),
        [SMEM] + [VMEM] * len(blocks), (VMEM, VMEM, VMEM), 16,
        flops=2 * width * width * rows, moved=4 * width * rows,
    )(place, *blocks)


def turn_kernel(full, out):
    step = 2 * TILE
    for k in range(full.shape[1] // step):
        out[k * step : (k + 1) * step, :] = full[:, k * step : (k + 1) * step].astype(F32).T.astype(BF16)


def turn(full):
    width, rows = full.shape
    return call(turn_kernel, shape((rows, width), BF16), [VMEM], VMEM, 16, moved=4 * width * rows)(full)


def pair_lhs(place, sources, lhs):
    odd = lax.rem(place[0], 2)
    for k, source in enumerate(sources):
        deep = source.shape[0]
        lhs[pl.ds(pl.multiple_of((odd ^ k) * deep, deep), deep), :] = source[...]


def rest_lhs(place, sources, lhs):
    (full,) = sources
    pair = lax.div(place[0], 2)
    across = full.shape[0] - lhs.shape[0]
    for k in range(lhs.shape[0] // across):
        q = k + (k >= pair).astype(jnp.int32)
        lhs[k * across : (k + 1) * across, :] = full[pl.ds(pl.multiple_of(q * across, across), across), :]


def cross_send_kernel(prepare, steps, place, *refs):
    *sources, active, out, lhs = refs
    wide = out.shape[1] // steps
    prepare(place, sources, lhs)

    for i in range(steps):
        source = pl.ds(pl.multiple_of((1 - place[1]) * out.shape[1] + i * wide, wide), wide)
        out[:, i * wide : (i + 1) * wide] = dot(lhs[...], active[:, source], ((1,), (0,))).astype(out.dtype)


def cross_send(prepare, deep, place, sources, active):
    rows, columns = active.shape
    return call(
        functools.partial(cross_send_kernel, prepare, 4), shape((deep, columns // 2), BF16),
        [SMEM] + [VMEM] * (len(sources) + 1), VMEM, 8,
        flops=deep * rows * columns, moved=rows * columns, scratch=(pltpu.VMEM((deep, rows), BF16),),
    )(place, *sources, active)


def cross_keep_kernel(prepare, chips, place, *refs):
    *sources, got, active = refs[: -1 - chips]
    outs, lhs = refs[-1 - chips : -1], refs[-1]
    wide = outs[0].shape[1]
    prepare(place, sources, lhs)
    for s, out in enumerate(outs):
        chunk = place[2] ^ s
        source = pl.ds(pl.multiple_of((place[1] * chips + chunk) * wide, wide), wide)
        where = pl.ds(pl.multiple_of(chunk * wide, wide), wide)
        total = dot(lhs[...], active[:, source], ((1,), (0,))) + got[:, where].astype(F32)
        out[...] = total.astype(out.dtype)


def cross_keep(prepare, deep, place, sources, got, active, chips):
    rows, columns = active.shape
    dims = (deep, columns // (2 * chips))
    return call(
        functools.partial(cross_keep_kernel, prepare, chips),
        [shape(dims, F32)] + [shape(dims, BF16)] * (chips - 1),
        [SMEM] + [VMEM] * (len(sources) + 2), [VMEM] * chips, 8,
        flops=deep * rows * columns, moved=rows * columns, scratch=(pltpu.VMEM((deep, rows), BF16),),
    )(place, *sources, got, active)


def swap(value, bit, rows):
    return lax.ppermute(value, "row", [(i, i ^ bit) for i in range(rows)])


def tree(values):
    values = [v.astype(F32) for v in values]
    while len(values) > 1:
        values = [a + b for a, b in zip(values[::2], values[1::2])]
    return values[0]


def bits_of(rows):
    return [1 << k for k in range(1, rows.bit_length() - 1)]


def reduce_cross(own, outs, rows):
    parts = [own] + [swap(v, 2 * s, rows) for s, v in enumerate(outs, 1)]
    return tree(parts).astype(BF16)


def gather_slow(mine, rows):
    stack = mine[None]
    for bit in bits_of(rows):
        other = swap(stack, bit, rows)
        stack = jnp.concatenate([stack, other], 0)
    return stack


def gather_fast(mine, rows):
    return [mine] + [swap(mine, 2 * s, rows) for s in range(1, rows // 2)]


def reduce_gram(keep, send, rows):
    own = keep + swap(send, 1, rows)
    parts = [own] + [swap(own, 2 * s, rows) for s in range(1, rows // 2)]
    total = tree(parts)
    return total, swap(total, 1, rows)


def spread(value, r):
    return jnp.broadcast_to(value[r : r + 1, :], (8, 128))


def eliminate(value, size):
    sub = lax.broadcasted_iota(jnp.int32, (8, 128), 0)
    lanes = range(value.shape[1] // 128)
    count = size // 8
    span = min(BAND, count)
    x = [[value[8 * q : 8 * q + 8, 128 * n : 128 * n + 128] for n in lanes] for q in range(count)]
    done = []
    for begin in range(0, count, span):
        end = begin + span
        band = []
        for t in range(begin, end):
            group, at = divmod(8 * t, 128)
            lead = [
                [jnp.broadcast_to(x[q][group][:, at + c : at + c + 1], (8, 128)) for c in range(8)]
                for q in range(t, end)
            ]
            out = [jnp.zeros((8, 128), F32) for _ in lanes]
            for r in range(8):
                root = lax.rsqrt(spread(lead[0][r], r))
                inverse = root * root
                rows = [spread(x[t][n], r) for n in lanes]
                out = [jnp.where(sub == r, v * root, o) for v, o in zip(rows, out)]
                rows = [v * inverse for v in rows]
                later = [spread(lead[0][c], r) * inverse for c in range(r + 1, 8)]
                for k, q in enumerate(range(t, end)):
                    column = lead[k][r]
                    if k == 0:
                        column = jnp.where(sub > r, column, 0.0)
                    for c in range(r + 1, 8):
                        lead[k][c] = lead[k][c] - column * later[c - r - 1]
                    x[q] = [a - column * v for a, v in zip(x[q], rows)]
            band.append(jnp.concatenate(out, 1))
        band = jnp.concatenate(band, 0)
        done.append(band)
        if end < count:
            change = exact(band[:, :size].T[8 * end :, :], band, ((1,), (0,)))
            for q in range(end, count):
                k = 8 * (q - end)
                x[q] = [x[q][n] - change[k : k + 8, 128 * n : 128 * n + 128] for n in lanes]
    return jnp.concatenate(done, 0)


def factor_first_kernel(place, mine, theirs, first, rest, whole):
    core = place[1]
    h = mine.shape[0]
    whole[pl.ds(pl.multiple_of(core * h, h), h), :] = mine[...]
    whole[pl.ds(pl.multiple_of((1 - core) * h, h), h), :] = theirs[...]
    line = lax.broadcasted_iota(jnp.int32, (h, h), 0)
    lane = lax.broadcasted_iota(jnp.int32, (h, h), 1)
    eye = (line == lane).astype(F32)
    value = eliminate(jnp.concatenate([whole[:h, :], eye], 1), h)
    first[...] = value
    r12 = value[:, h : 2 * h]
    rest[...] = whole[h:, h:] - exact(r12, r12, ((0,), (0,)))


def factor_last_kernel(first, rest, triangle, inverse, turned):
    h = first.shape[0]
    line = lax.broadcasted_iota(jnp.int32, (h, h), 0)
    lane = lax.broadcasted_iota(jnp.int32, (h, h), 1)
    eye = (line == lane).astype(F32)
    zero = jnp.zeros((h, h), F32)
    second = eliminate(jnp.concatenate([rest[...], eye], 1), h)
    r11, r12, i11 = first[:, :h], first[:, h : 2 * h], first[:, 2 * h :]
    r22, i22 = second[:, :h], second[:, h:]
    i11 = jnp.where(lane <= line, i11, 0.0)
    i22 = jnp.where(lane <= line, i22, 0.0)
    i21 = -exact(i22, exact(r12, i11, ((0,), (0,))), ((1,), (0,)))
    triangle[:h, :h] = jnp.where(lane >= line, r11, 0.0)
    triangle[:h, h:] = r12
    triangle[h:, :h] = zero
    triangle[h:, h:] = jnp.where(lane >= line, r22, 0.0)
    full = jnp.concatenate([jnp.concatenate([i11, zero], 1), jnp.concatenate([i21, i22], 1)], 0)
    inverse[0], inverse[1] = split(full)
    turned[0], turned[1] = split(full.T)


def factor_first(place, mine, theirs):
    h, size = mine.shape
    return call(
        factor_first_kernel, (shape((h, 3 * h), F32), shape((h, h), F32)), [SMEM, VMEM, VMEM],
        (VMEM,) * 2, 8, flops=10 * size**3, moved=20 * MIB, scratch=(pltpu.VMEM((size, size), F32),),
    )(place, mine, theirs)


def factor_last(first, rest):
    size = 2 * first.shape[0]
    both = shape((2, size, size), BF16)
    return call(
        factor_last_kernel, (shape((size, size), F32), both, both), [VMEM, VMEM], (VMEM,) * 3, 8,
        flops=10 * size**3, moved=20 * MIB,
    )(first, rest)


def coeff_kernel(place, inverse, turned, one, *refs):
    *several, top_out, coeff_out, sums = refs
    pair = lax.div(place[0], 2)
    two, wide = one.shape[1:]
    straight = ((1,), (0,))
    for s, other in enumerate(several):
        sums[s % 2, pl.ds(pl.multiple_of(pair * two, two), two), :] = one[s]
        for k in range(other.shape[0] // two):
            q = k + (k >= pair).astype(jnp.int32)
            sums[s % 2, pl.ds(pl.multiple_of(q * two, two), two), :] = other[k * two : (k + 1) * two, :]
        cross = sums[s % 2]
        top = dot(inverse[0], cross, straight) + dot(inverse[1], cross, straight)
        high, low = split(top)
        part = slice(s * wide, (s + 1) * wide)
        top_out[part, :] = top.T
        coeff_out[:, part] = (
            dot(turned[0], high, straight) + (dot(turned[0], low, straight) + dot(turned[1], high, straight))
        ).astype(BF16)


def coefficients(place, inverse, turned, one, several):
    size = inverse.shape[1]
    wide = one.shape[2]
    half = wide * len(several)
    return call(
        coeff_kernel, (shape((half, size), F32), shape((size, half), BF16)),
        [SMEM] + [VMEM] * (3 + len(several)), (VMEM, VMEM), 12,
        flops=10 * size * size * half, moved=8 * size * half, scratch=(pltpu.VMEM((2, size, wide), BF16),),
    )(place, inverse, turned, one, *several)


def update_kernel(chips, mine, place, panel, coeff, top, active, *refs):
    top_out, out, results, top_sem, out_sems = refs[-5:]
    chip = place[2]
    side = place[1] if mine else 1 - place[1]
    rows, wide = results.shape[1:]
    block = rows // 4

    def where(s):
        return pl.ds(pl.multiple_of((side * chips + (chip ^ s)) * wide, wide), wide)

    def top_copy(s):
        return pltpu.make_async_copy(top.at[pl.ds(s * wide, wide), :], top_out.at[where(s), :], top_sem)

    def out_copy(s, part):
        return pltpu.make_async_copy(results.at[s % 2, part, :], out.at[part, where(s)], out_sems.at[s % 2])

    for s in range(chips):
        top_copy(s).start()
    for s in range(chips):
        if s >= 2:
            out_copy(s - 2, pl.ds(0, rows)).wait()
        weights = coeff[:, s * wide : (s + 1) * wide]
        for k in range(0, rows, block):
            product = dot(panel[k : k + block, :], weights, ((1,), (0,)))
            results[s % 2, k : k + block, :] = (active[k : k + block, where(s)].astype(F32) - product).astype(BF16)
            out_copy(s, pl.ds(k, block)).start()
    for s in range(max(chips - 2, 0), chips):
        out_copy(s, pl.ds(0, rows)).wait()
    half = chips * wide
    pltpu.make_async_copy(top, top_out.at[pl.ds(0, half), :], top_sem).wait()


def update(mine, chips, place, panel, coeff, top, active, before=()):
    rows, size = panel.shape
    columns = active.shape[1]
    wide = columns // (2 * chips)
    return call(
        functools.partial(update_kernel, chips, mine),
        (shape((columns, size), F32), shape((rows, columns), BF16)),
        [SMEM] + [VMEM] * 4 + [ANY] * len(before), (ANY, ANY), 12,
        flops=rows * size * columns, moved=rows * columns,
        scratch=(
            pltpu.VMEM((2, rows, wide), BF16),
            pltpu.SemaphoreType.DMA(()),
            pltpu.SemaphoreType.DMA((2,)),
        ),
        aliases={5: 0, 6: 1} if before else None,
    )(place, panel, coeff, top, active, *before)


def gather_panel(own, ncol):
    def shift(value, pairs):
        return lax.ppermute(value, "col", pairs)

    def direct(s):
        return shift(own, [(i, i ^ s) for i in range(ncol)])

    if ncol != 4:
        return [own] + [direct(s) for s in range(1, ncol)]
    across = direct(2)
    return [own, direct(1), across, shift(own, [(1, 2), (2, 1)]), shift(across, [(2, 3), (1, 0)])]


def local(nrow, ncol, panel, trailing, tile_list):
    row = lax.axis_index("row")
    place = jnp.stack([lax.axis_index("col"), row % 2, row // 2]).astype(jnp.int32)
    chips = nrow // 2
    own = pick(tile_list, panel.T)
    blocks = gather_panel(own, ncol)
    across = 2 * panel.shape[1]
    active = load(tile_list, trailing)

    def both(prepare, deep, sources):
        got = swap(cross_send(prepare, deep, place, sources, active), 1, nrow)
        own, *outs = cross_keep(prepare, deep, place, sources, got, active, chips)
        return reduce_cross(own, outs, nrow)

    one = gather_slow(both(pair_lhs, across, blocks[:2]), nrow)
    full, keep, send = gram(place, blocks, ncol)
    sums = reduce_gram(keep, send, nrow)
    turned_panel = turn(full)
    two = gather_fast(both(rest_lhs, (ncol - 2) * panel.shape[1], [full]), nrow)
    triangle, inverse, turned = factor_last(*factor_first(place, *sums))
    top, coeff = coefficients(place, inverse, turned, one, two)
    outs = update(True, chips, place, turned_panel, coeff, top, active)
    coeff, top = swap(coeff, 1, nrow), swap(top, 1, nrow)
    top_rows, updated = update(False, chips, place, turned_panel, coeff, top, active, outs)
    return triangle, top_rows, updated


def solution(mesh):
    nrow, ncol = mesh.shape["row"], mesh.shape["col"]

    def program(panel, trailing, tile_list):
        return local(nrow, ncol, panel, trailing, tile_list)

    return jax.shard_map(
        program,
        mesh=mesh,
        in_specs=(P("row", "col"), P("row", "col"), P("row")),
        out_specs=(P(), P("col", None), P("row", "col")),
        check_vma=False,
    )
```
